32 devices in a mesh: lat: 4 (over z), lev: 8 (over y, x, core).
Axes of the slice: x: 2, y: 2, z: 4, core: 2. Of those that a mesh axis runs over, the one named last changes fastest.
Arguments:
- spec_in: bfloat16 [8, 2, 8, 2560], P('lat', None, None, 'lev'), may hold values from -6 to 6
- legendre: bfloat16 [8, 2560, 2560], P('lat', 'lev'), may hold values from -0.125 to 0.125
- pattern: int32 [8, 20, 20], P('lat'), may hold values from 0 to 1, as said below
- deal_list: int32 [8], replicated, may hold values from 0 to 2559, as said below
- circle_lengths: int32 [2560], replicated, may hold values from 12 to 10256, as said below
- mixing: bfloat16 [8, 8], replicated, may hold values from -2 to 2
Outputs:
- spec_out: float32 [8, 2, 8, 2560], P('lat', None, None, 'lev')
The draws below stay inside these ranges and needn't reach their ends.
Inputs may be any that keep to these rules, and one draw needn't show every extreme that they name: `deal_list`: distinct wavenumbers; 0 and 2559 are always among them. pattern[m, a, b] is 1 exactly when b * 128 <= 2559 - deal_list[m] and a >= (deal_list[m] * 20) // 5120, else 0. `circle_lengths`: multiples of 4; row j holds a value between 20 + 4 j - 4 (j // 2 + 2) and 20 + 4 j, and the last row exactly 20 + 4 (2559).
All inputs are finite; a program needn't handle non-finite values.
Results may differ from the reference program's by a relative error of at most 0.0026.
Values may be sent and summed in bfloat16 or wider, within the bound.
A program may use at most 64 MiB of HBM per device.

```python
import math
import jax
import jax.numpy as jnp
from jax import lax

NLAT = 5120
NK = 2560
BLK = 128
HLAT = 2560
MW = 8
FIELDS = 8


def common_waves(key):
    first_key = jax.random.fold_in(key, 11)
    second_key = jax.random.fold_in(key, 12)
    middle = 1 + jax.random.permutation(first_key, NK - 2)[:MW - 2]
    chosen = jnp.concatenate([jnp.array([0, NK - 1], dtype=jnp.int32), middle.astype(jnp.int32)])
    return jax.random.permutation(second_key, chosen)


def draw_deal_list(key, part):
    return common_waves(key)


def draw_pattern(key, part):
    wavenums = common_waves(key)
    row_blocks = jnp.arange(HLAT // BLK, dtype=jnp.int32)
    col_blocks = jnp.arange(NK // BLK, dtype=jnp.int32)
    polar_cut = wavenums * (HLAT // BLK) // (2 * NK)
    rows_live = row_blocks[None, :] >= polar_cut[:, None]
    cols_live = col_blocks[None, :] * BLK <= (NK - 1 - wavenums)[:, None]
    return (rows_live[:, :, None] & cols_live[:, None, :]).astype(jnp.int32)


def draw_circle_lengths(key, part):
    row_ids = jnp.arange(HLAT, dtype=jnp.int32)
    upper = (row_ids // 2 + 3).astype(jnp.int32)
    dropped = jax.random.randint(jax.random.fold_in(key, 21), (HLAT,), 0, upper).astype(jnp.int32)
    dropped = jnp.where(row_ids == HLAT - 1, 0, dropped)
    return (20 + 4 * row_ids - 4 * dropped).astype(jnp.int32)


def steps_of(stream_key, shape, split, smallest, largest):
    loudness, own = 1.0, jax.random.fold_in(stream_key, 6)
    for dim, shards_of in split:
        heights = jnp.exp(jax.random.uniform(jax.random.fold_in(own, dim), (shards_of,), jnp.float32, smallest / len(split), largest / len(split)))
        loudness = loudness * jnp.repeat(heights, shape[dim] // shards_of).reshape([-1 if axis == dim else 1 for axis in range(len(shape))])
    return loudness


def normal_values(own_key, dims, spread, most, shards=(), kind=jnp.bfloat16):
    values = jax.random.normal(own_key, dims, jnp.float32) * spread
    if len(shards) > 0:
        values = steps_of(own_key, dims, shards, -0.22, 0.18) * values
    return jnp.clip(values, min=-most, max=most).astype(kind)


def setup_inputs(seed: int = 0) -> dict:
    seeds = jax.random.split(jax.random.key(seed), 7)
    spec_in = normal_values(seeds[0], (MW, 2, FIELDS, NK), 1.0, 6.0, ((0, 4), (3, 8)))
    legendre = normal_values(seeds[1], (MW, NK, HLAT), NK ** -0.5, 0.125, ((0, 4), (1, 8)))
    pattern = draw_pattern(jax.random.fold_in(seeds[6], 71), 0)
    deal_list = draw_deal_list(jax.random.fold_in(seeds[6], 71), 0)
    circle_lengths = draw_circle_lengths(jax.random.fold_in(seeds[6], 71), 0)
    mixing = normal_values(seeds[5], (FIELDS, FIELDS), FIELDS ** -0.5, 2.0)
    return {"spec_in": spec_in, "legendre": legendre, "pattern": pattern, "deal_list": deal_list, "circle_lengths": circle_lengths, "mixing": mixing}


def live_table(block_mask, dense_rows):
    expanded = jnp.repeat(jnp.repeat(block_mask, BLK, axis=0), BLK, axis=1)
    return dense_rows.astype(jnp.float32) * jnp.transpose(expanded).astype(jnp.float32)

def circle_tables(wavenums, length):
    lon_count = 20 + 4 * (HLAT - 1)
    positions = jnp.arange(lon_count, dtype=jnp.int32)
    phases = wavenums.astype(jnp.int32)[:, None] * positions[None, :] % length
    angles = phases.astype(jnp.float32) * (2.0 * math.pi) / length.astype(jnp.float32)
    inside = positions[None, :] < length
    cosine_table = jnp.where(inside, jnp.cos(angles), 0.0).astype(jnp.bfloat16)
    sine_table = jnp.where(inside, jnp.sin(angles), 0.0).astype(jnp.bfloat16)
    return (cosine_table, sine_table)

def reference(spec_in, legendre, pattern, deal_list, circle_lengths, mixing):
    parity = (1 - 2 * (jnp.arange(NK, dtype=jnp.int32) % 2)).astype(jnp.float32)

    def inverse_one(inputs):
        dense_rows, block_mask, coeffs = inputs
        masked = live_table(block_mask, dense_rows)
        coeff_f = coeffs.astype(jnp.float32)
        stacked = jnp.stack([coeff_f, coeff_f * parity], axis=0)
        return jnp.einsum('kj,hrfk->hrfj', masked, stacked).astype(jnp.bfloat16)
    fourier = lax.map(inverse_one, (legendre, pattern, spec_in))
    rows_first = jnp.moveaxis(fourier, 4, 0)
    mixing_f = mixing.astype(jnp.float32)
    synth_scale = (2.0 * MW) ** (-0.5)

    def row_one(inputs):
        fourier_row, row_id = inputs
        length = circle_lengths[row_id]
        cosine_table, sine_table = circle_tables(deal_list, length)
        phases_table = jnp.concatenate([cosine_table, -sine_table], axis=0).astype(jnp.float32)
        coeffs = jnp.transpose(fourier_row, (1, 3, 2, 0)).reshape(2 * FIELDS, 2 * MW).astype(jnp.float32)
        grid_values = (jnp.dot(coeffs, phases_table) * synth_scale).astype(jnp.bfloat16)
        grid_f = grid_values.astype(jnp.float32).reshape(2, FIELDS, -1)
        mixed_sum = jnp.einsum('fg,hgl->hfl', mixing_f, grid_f)
        column = (grid_f + jnp.tanh(mixed_sum)).astype(jnp.bfloat16).reshape(2 * FIELDS, -1)
        weight = jnp.sin(math.pi * (row_id.astype(jnp.float32) + 0.5) / NLAT) / jnp.sqrt(length.astype(jnp.float32))
        analysis = (jnp.dot(column.astype(jnp.float32), phases_table.T) * weight).astype(jnp.bfloat16)
        return jnp.transpose(analysis.reshape(2, FIELDS, 2, MW), (3, 0, 2, 1))
    analysed = lax.map(row_one, (rows_first, jnp.arange(HLAT, dtype=jnp.int32)))
    analysed = jnp.moveaxis(analysed, 0, 4)

    def direct_one(inputs):
        dense_rows, block_mask, coeffs = inputs
        masked = live_table(block_mask, dense_rows)
        product = jnp.einsum('kj,hrfj->hrfk', masked, coeffs.astype(jnp.float32))
        return product[0] + parity * product[1]
    return lax.map(direct_one, (legendre, pattern, analysed))
```

```python
import functools
import math

import jax
import jax.numpy as jnp
from jax import lax
from jax.experimental import pallas as pl
from jax.experimental.pallas import tpu as pltpu
from jax.sharding import PartitionSpec as P

BLK = 128
SPAN = 2 * BLK
STREAMS = 2


def iota(shape, axis):
    return lax.broadcasted_iota(jnp.int32, shape, axis)


def unit(condition):
    return jnp.where(condition, 1.0, 0.0).astype(jnp.float32)


class Plan:
    def __init__(self, waves, fields, lat_count, lev_count, half_lat):
        self.waves, self.fields = waves, fields
        self.half_lat = half_lat
        self.devices = lat_count * lev_count
        self.rows = half_lat // self.devices
        self.hf = 2 * fields
        self.lanes = waves * 4 * fields
        self.share = max(
            n for n in range(1, self.rows + 1) if self.rows % n == 0 and (n == 1 or 4 * n * waves <= BLK)
        )
        self.groups = self.rows // self.share
        self.block = self.share * waves
        self.depth = 4 * self.block
        self.images = self.share * self.hf
        self.scale = (2.0 * waves) ** (-0.5)

    def tiles(self, group):
        last = ((group + 1) * self.share - 1) * self.devices + self.devices - 1
        return -(-(last + 6) // SPAN)

    def inside(self, group, tile):
        first = group * self.share * self.devices
        return (tile + 1) * SPAN - 1 < 3 + first - first // 2

    def scratch(self):
        return [
            pltpu.VMEM((self.groups, 4 * self.images, self.depth), jnp.bfloat16),
            pltpu.VMEM((self.groups, 4, self.block, BLK), jnp.float32),
            pltpu.VMEM((self.groups * 2 * self.block, 4 * self.images), jnp.float32),
            pltpu.VMEM((self.rows, BLK), jnp.float32),
        ]


def waves_at(deal, index, waves):
    out = jnp.zeros_like(index)
    for wave in range(waves):
        out = jnp.where(index == wave, deal[wave], out)
    return out


def fill_tables(plan, device, lengths, deal, table, row_length):
    wave = waves_at(deal, iota((plan.block, BLK), 0) % plan.waves, plan.waves).astype(jnp.float32)
    product = wave * iota((plan.block, BLK), 1).astype(jnp.float32)
    member = iota((plan.block, 1), 0) // plan.waves

    def fill(group, carry):
        length = jnp.zeros((plan.block, 1), jnp.float32)
        for each in range(plan.share):
            own = lengths[(group * plan.share + each) * plan.devices + device].astype(jnp.float32)
            length = jnp.where(member == each, own, length)
            row_length[pl.ds(group * plan.share + each, 1), :] = jnp.full((1, BLK), own, jnp.float32)
        turned = product - jnp.floor(product / length) * length
        angle = turned * (2.0 * math.pi) / length
        cosine, sine = jnp.cos(angle), jnp.sin(angle)
        last_cos, last_sin = cosine[:, BLK - 1 : BLK], sine[:, BLK - 1 : BLK]
        next_cos, next_sin = cosine[:, 1:2], sine[:, 1:2]
        table[group, 0] = cosine
        table[group, 1] = -sine
        table[group, 2] = jnp.broadcast_to(last_cos * next_cos - last_sin * next_sin, product.shape)
        table[group, 3] = jnp.broadcast_to(-last_sin * next_cos - last_cos * next_sin, product.shape)
        return carry

    lax.fori_loop(0, plan.groups, fill, 0)


def lane_waves(plan, deal):
    return waves_at(deal, iota((1, plan.lanes), 1) // (4 * plan.fields), plan.waves)


def live_rows(plan, device, deal):
    half_lat = plan.half_lat
    cut = lane_waves(plan, deal) * (half_lat // BLK) // (2 * half_lat)
    row = iota((plan.rows, 1), 0) * plan.devices + device
    return unit(row // BLK >= cut)


def image_sign(image, sine, odd):
    sign = jnp.ones(jnp.broadcast_shapes(sine.shape, odd.shape), jnp.float32)
    if image % 2:
        sign = sign * (1.0 - 2.0 * unit(sine))
    if image // 2:
        sign = sign * (1.0 - 2.0 * unit(odd))
    return sign


def mix_fields(plan, values, mixing_ref):
    fields = plan.fields
    pick = unit(iota((BLK, fields), 0) % fields == iota((BLK, fields), 1)).astype(jnp.bfloat16)
    across = (((1,), (1,)), ((), ()))
    half = lax.dot_general(
        pick, mixing_ref[...], across, preferred_element_type=jnp.float32
    ).astype(jnp.bfloat16)
    mixer = lax.dot_general(half, pick, across, preferred_element_type=jnp.float32)
    same = iota((BLK, BLK), 0) // fields == iota((BLK, BLK), 1) // fields
    mixer = jnp.where(same, mixer, 0.0).astype(jnp.bfloat16)
    return jnp.concatenate(
        [
            jnp.dot(values[:, at : at + BLK], mixer, preferred_element_type=jnp.float32)
            for at in range(0, plan.lanes, BLK)
        ],
        axis=1,
    )


def place_coefficients(plan, values, deal, mixing_ref, left):
    waves, fields, hf, lanes = plan.waves, plan.fields, plan.hf, plan.lanes
    mixed = plan.scale * mix_fields(plan, values, mixing_ref)
    high = mixed.astype(jnp.bfloat16).astype(jnp.float32)
    lane = iota((hf, lanes), 1)
    keep = unit(lane // (2 * fields) % 2 * fields + lane % fields == iota((hf, lanes), 0))
    rows = values.shape[0]
    spread = jnp.concatenate(
        [
            (source[:, None, :] * keep[None, :, :]).reshape(rows * hf, lanes).astype(jnp.bfloat16)
            for source in (high, mixed - high)
        ],
        axis=1,
    )
    down, right = iota((2 * lanes, plan.depth), 0), iota((2 * lanes, plan.depth), 1)
    down_kind = down // lanes * 2 + down % lanes // fields % 2
    down_wave = down % lanes // (4 * fields)
    gather = unit((down_kind == right // plan.block) & (down_wave == right % waves)).astype(jnp.bfloat16)
    placed = jnp.dot(spread, gather, preferred_element_type=jnp.float32)
    right = iota((1, plan.depth), 1)
    mine = unit(iota((plan.images, 1), 0) // hf == right % plan.block // waves)
    odd = waves_at(deal, right % waves, waves) % 2 == 1
    sine = right // plan.block % 2 == 1
    signs = [mine * image_sign(image, sine, odd) for image in range(4)]
    for group in range(rows // plan.share):
        own = placed[group * plan.images : (group + 1) * plan.images]
        for image in range(4):
            left[group, image * plan.images : (image + 1) * plan.images, :] = (
                own * signs[image]
            ).astype(jnp.bfloat16)


def walk_circles(plan, groups, device, lengths, table, left, total):
    position = iota((1, SPAN), 1)
    member = iota((plan.block, 1), 0) // plan.waves
    across = (((1,), (1,)), ((), ()))

    def phases(group, tile, cos_now, sin_now):
        step_cos, step_sin = table[group, 2], table[group, 3]
        cosines, sines = [], []
        for _ in range(SPAN // BLK):
            cosines.append(cos_now)
            sines.append(sin_now)
            cos_now, sin_now = (
                cos_now * step_cos - sin_now * step_sin,
                sin_now * step_cos + cos_now * step_sin,
            )
        cosine, sine = jnp.concatenate(cosines, axis=1), jnp.concatenate(sines, axis=1)
        near, far = cosine.astype(jnp.bfloat16), sine.astype(jnp.bfloat16)
        weights = jnp.concatenate([near, far, near, far], axis=0)
        if tile > 0 and plan.inside(group, tile):
            return cos_now, sin_now, weights, weights[: 2 * plan.block]
        at = position + tile * SPAN
        quarter = jnp.zeros((plan.block, 1), jnp.int32)
        for each in range(plan.share):
            own = lengths[(group * plan.share + each) * plan.devices + device]
            quarter = jnp.where(member == each, lax.shift_right_logical(own, 2), quarter)
        share = jnp.where(at < quarter, 1.0, jnp.where(at == quarter, 0.5, 0.0)).astype(jnp.float32)
        if tile == 0:
            share = share * jnp.where(at == 0, 0.5, 1.0).astype(jnp.float32)
        shared = jnp.concatenate([cosine * share, sine * share], axis=0).astype(jnp.bfloat16)
        return cos_now, sin_now, weights, shared

    streams = [[] for _ in range(STREAMS)]
    for group in sorted(groups, key=lambda group: -plan.tiles(group)):
        min(streams, key=len).extend((group, tile) for tile in range(plan.tiles(group)))
    state, sums, waiting = {}, {}, []

    def finish():
        for group, shared, grid in waiting:
            extra = lax.dot_general(
                shared,
                jnp.tanh(grid).astype(jnp.bfloat16),
                across,
                preferred_element_type=jnp.float32,
            )
            sums[group] = sums[group] + extra if group in sums else extra
        waiting.clear()

    for step in range(max(len(stream) for stream in streams)):
        started = []
        for stream in streams:
            if step < len(stream):
                group, tile = stream[step]
                if group not in state:
                    state[group] = table[group, 0], table[group, 1]
                cos_now, sin_now, weights, shared = phases(group, tile, *state[group])
                state[group] = cos_now, sin_now
                grid = jnp.dot(left[group], weights, preferred_element_type=jnp.float32)
                started.append((group, shared, grid))
        finish()
        waiting.extend(started)
    finish()
    size = 2 * plan.block
    for group in groups:
        total[group * size : (group + 1) * size, :] = sums[group]


def fold_circles(plan, sums, deal):
    waves, fields, hf, lanes = plan.waves, plan.fields, plan.hf, plan.lanes
    size, wide = 2 * plan.block, 4 * plan.images
    down, right = iota((size, wide), 0), iota((size, wide), 1)
    odd = waves_at(deal, down % waves, waves) % 2 == 1
    sine = down // plan.block == 1
    sign = jnp.zeros((size, wide), jnp.float32)
    for image in range(4):
        sign = jnp.where(right // plan.images == image, image_sign(image, sine, odd), sign)
    sign = sign * unit(down % plan.block // waves == right % plan.images // hf)
    count = sums.shape[0] // size
    signed = (sums.reshape(count, size, wide) * sign[None]).reshape(count * size, wide)
    high = signed.astype(jnp.bfloat16)
    low = (signed - high.astype(jnp.float32)).astype(jnp.bfloat16)
    down, right = iota((2 * wide, lanes), 0), iota((2 * wide, lanes), 1)
    spread = unit(down % hf == right // (2 * fields) % 2 * fields + right % fields).astype(jnp.bfloat16)
    folded = jnp.dot(
        jnp.concatenate([high, low], axis=1), spread, preferred_element_type=jnp.float32
    )
    down, right = iota((size, lanes), 0), iota((size, lanes), 1)
    keep = unit((down // plan.block == right // fields % 2) & (down % waves == right // (4 * fields)))
    kept = (folded.reshape(count, size, lanes) * keep[None]).reshape(count, 2, plan.share, waves, lanes)
    return jnp.sum(jnp.sum(kept, axis=1), axis=2).reshape(count * plan.share, lanes)


def circle_products(plan, values, length, deal):
    waves, lanes = plan.waves, plan.lanes
    wave = lane_waves(plan, deal).astype(jnp.float32)
    part = 1.0 - 2.0 * unit(iota((1, lanes), 1) // plan.fields % 2 == 1)
    inverse = 1.0 / length

    def whole(turns):
        return unit(turns == length * jnp.floor(turns * inverse + 0.5))

    out = jnp.zeros_like(values)
    for other in range(waves):
        at = other * 4 * plan.fields

        def turn(source):
            return jnp.concatenate([source[:, at:], source[:, :at]], axis=1) if at else source

        partner = turn(wave)
        gram = whole(wave - partner) + part * whole(wave + partner)
        out = out + gram * turn(values)
    return out * (0.5 * plan.scale) * length


def row_kernel(lengths, deal, fourier_ref, mixing_ref, out_ref, left, table, total, row_length):
    lat_count, count, block_width = fourier_ref.shape
    fields = mixing_ref.shape[0]
    plan = Plan(deal.shape[0], fields, lat_count, lax.axis_size("lev"), lengths.shape[0])
    rows = plan.rows
    pack = rows // count
    part_span = block_width // pack
    device = lax.axis_index("lev") * lat_count + lax.axis_index("lat")
    fill_tables(plan, device, lengths, deal, table, row_length)
    blocks = [fourier_ref[side].astype(jnp.float32) for side in range(lat_count)]
    values = jnp.concatenate(
        [
            jnp.concatenate(
                [block[:, part * part_span : (part + 1) * part_span] for block in blocks], axis=1
            )
            for part in range(pack)
        ],
        axis=0,
    )
    live = live_rows(plan, device, deal)
    values = values * live
    place_coefficients(plan, values.astype(jnp.bfloat16), deal, mixing_ref, left)
    walk_circles(plan, range(plan.groups), device, lengths, table, left, total)
    summed = fold_circles(plan, total[...], deal)
    length = jnp.concatenate([row_length[...]] * (plan.lanes // BLK), axis=1)
    row = (iota((rows, 1), 0) * plan.devices + device).astype(jnp.float32)
    weight = jnp.sin(math.pi * (row + 0.5) / (2 * plan.half_lat)) / jnp.sqrt(length)
    summed = (summed + circle_products(plan, values, length, deal)) * (weight * live)
    for side in range(lat_count):
        out_ref[side] = jnp.concatenate(
            [
                summed[
                    part * count : (part + 1) * count, side * part_span : (side + 1) * part_span
                ]
                for part in range(pack)
            ],
            axis=1,
        ).astype(jnp.bfloat16)


def rows_step(fourier, lengths, deal_list, mixing):
    lat_count, lev_count = lax.axis_size("lat"), lax.axis_size("lev")
    plan = Plan(deal_list.shape[0], mixing.shape[0], lat_count, lev_count, lengths.shape[0])
    vmem = pl.BlockSpec(memory_space=pltpu.VMEM)
    smem = pl.BlockSpec(memory_space=pltpu.SMEM)
    return pl.pallas_call(
        row_kernel,
        out_shape=jax.ShapeDtypeStruct(fourier.shape, jnp.bfloat16),
        in_specs=[smem, smem, vmem, vmem],
        out_specs=vmem,
        scratch_shapes=plan.scratch(),
    )(lengths, deal_list, fourier, mixing)


def column_masks(pattern_ref, local_cols):
    slots, blocks_down, blocks = pattern_ref.shape
    column = lax.broadcasted_iota(jnp.int32, (1, local_cols), 1)
    column = column + lax.axis_index("lev") * local_cols
    odd = (1 - 2 * (column % 2)).astype(jnp.float32)
    masks = []
    for slot in range(slots):
        mask = jnp.zeros((1, local_cols), jnp.float32)
        for block in range(blocks):
            kept = pattern_ref[slot, blocks_down - 1, block].astype(jnp.float32)
            mask = jnp.where(column // BLK == block, kept, mask)
        masks.append(mask)
    return odd, masks


def peers_of(axis):
    count = lax.axis_size(axis)
    return [lax.rem(lax.axis_index(axis) + off, count) for off in range(1, count)]


def greet():
    expect(hail())


def expect(total):
    pl.semaphore_wait(pltpu.get_barrier_semaphore(), total)


def hail():
    barrier = pltpu.get_barrier_semaphore()
    total = 0
    for axis in ("lat", "lev"):
        for peer in peers_of(axis):
            pl.semaphore_signal(
                barrier, inc=1, device_id={axis: peer}, device_id_type=pl.DeviceIdType.MESH
            )
            total += 1
    return total


def send(axis, sources, target, sems):
    copies = []
    for step, peer in enumerate(peers_of(axis)):
        copy = pltpu.make_async_remote_copy(
            src_ref=sources(peer),
            dst_ref=target,
            send_sem=sems.at[0, step],
            recv_sem=sems.at[1, step],
            device_id={axis: peer},
            device_id_type=pl.DeviceIdType.MESH,
        )
        copy.start()
        copies.append(copy)
    return copies


def inward_kernel(pack, pattern_ref, spec_ref, legendre_ref, out_ref, turned, leaving, arriving, summed, landed,
                  lev_sems, lat_sems):
    slots, _, half_lat = legendre_ref.shape
    lev_count, lat_count, count, width = leaving.shape
    devices = lev_count * lat_count
    lev_index, lat_index = lax.axis_index("lev"), lax.axis_index("lat")
    packed = half_lat // pack
    greetings = hail()
    odd, masks = column_masks(pattern_ref, legendre_ref.shape[1])
    sums = []
    for slot in range(slots):
        kept = jnp.concatenate([spec_ref[slot, 0], spec_ref[slot, 1]], axis=0).astype(jnp.float32)
        kept = kept * masks[slot]
        sums.append(
            jnp.dot(
                jnp.concatenate([kept, kept * odd], axis=0).astype(jnp.bfloat16),
                legendre_ref[slot],
                preferred_element_type=jnp.float32,
            )
        )
    for block in range(packed // BLK):
        piece = jnp.concatenate(
            [
                value[:, part * packed + block * BLK : part * packed + (block + 1) * BLK]
                for part in range(pack)
                for value in sums
            ],
            axis=0,
        )
        turned[:, block * BLK : (block + 1) * BLK, :] = jnp.stack(
            [piece[at : at + BLK].T for at in range(0, width, BLK)]
        )
    for device in range(devices):
        for at in range(width // BLK):
            leaving[device // lat_count, device % lat_count, :, at * BLK : (at + 1) * BLK] = (
                turned[at, pl.ds(device, count, stride=devices), :].astype(jnp.bfloat16)
            )
    expect(greetings)
    copies = send("lev", lambda peer: leaving.at[peer], arriving.at[lev_index], lev_sems)
    mine = lev_index * lat_count
    total = jnp.stack(
        [
            jnp.concatenate(
                [
                    turned[at, pl.ds(mine + side, count, stride=devices), :]
                    for at in range(width // BLK)
                ],
                axis=1,
            )
            for side in range(lat_count)
        ]
    )
    for copy, peer in zip(copies, [lax.rem(lev_index + lev_count - off, lev_count) for off in range(1, lev_count)]):
        copy.wait_recv()
        total = total + arriving[peer].astype(jnp.float32)
    summed[...] = total.astype(jnp.bfloat16)
    crossing = send("lat", lambda peer: summed.at[peer], landed.at[lat_index], lat_sems)
    out_ref[lat_index] = summed[lat_index]
    for copy, peer in zip(crossing, [lax.rem(lat_index + lat_count - off, lat_count) for off in range(1, lat_count)]):
        copy.wait_recv()
        out_ref[peer] = landed[peer]
    for copy in copies + crossing:
        copy.wait_send()


def outward_kernel(pack, fields, pattern_ref, rows_ref, legendre_ref, out_ref, held, landed, gathered, turned,
                   lev_sems, lat_sems, load_sem):
    slots, local_cols, half_lat = held.shape
    lev_count, lat_count, count, width = gathered.shape
    devices = lev_count * lat_count
    lev_index, lat_index = lax.axis_index("lev"), lax.axis_index("lat")
    packed = half_lat // pack
    part_width = 4 * fields
    load = pltpu.make_async_copy(legendre_ref, held, load_sem)
    load.start()
    greet()
    crossing = send("lat", lambda peer: rows_ref.at[peer], landed.at[lat_index], lat_sems)
    landed[lat_index] = rows_ref[lat_index]
    for copy in crossing:
        copy.wait_recv()
    copies = send("lev", lambda peer: landed, gathered.at[lev_index], lev_sems)
    gathered[lev_index] = landed[...]
    for copy in copies:
        copy.wait_recv()
    for device in range(devices):
        block = gathered[device // lat_count, device % lat_count].astype(jnp.float32)
        for at in range(width // BLK):
            turned[at, pl.ds(device, count, stride=devices), :] = block[:, at * BLK : (at + 1) * BLK]
    load.wait()
    odd, masks = column_masks(pattern_ref, local_cols)
    sides = [turned[at].astype(jnp.bfloat16) for at in range(width // BLK)]
    for slot in range(slots):
        total = None
        for part in range(pack):
            at = part * slots * part_width + slot * part_width
            value = jnp.dot(
                held[slot, :, part * packed : (part + 1) * packed],
                sides[at // BLK],
                preferred_element_type=jnp.float32,
            )[:, at % BLK : at % BLK + part_width]
            total = value if total is None else total + value
        flat = total.T
        joined = flat[: 2 * fields] + odd * flat[2 * fields :]
        out_ref[slot] = joined * masks[slot]
    for copy in copies + crossing:
        copy.wait_send()


def local(spec_in, legendre, pattern, deal_list, circle_lengths, mixing):
    lat_index = lax.axis_index("lat")
    lev_index = lax.axis_index("lev")
    lat_count = lax.axis_size("lat")
    lev_count = lax.axis_size("lev")
    slots, local_cols, half_lat = legendre.shape
    fields = spec_in.shape[2]
    devices = lat_count * lev_count
    rows = half_lat // devices
    span = 4 * slots * fields
    pack = max(1, BLK // span)
    count, width = rows // pack, span * pack
    vmem = pl.BlockSpec(memory_space=pltpu.VMEM)
    block_shape = (lat_count, count, width)
    sems = [
        pltpu.SemaphoreType.DMA((2, lev_count)),
        pltpu.SemaphoreType.DMA((2, lat_count)),
    ]
    turned = pltpu.VMEM((width // BLK, half_lat // pack, BLK), jnp.float32)
    fourier = pl.pallas_call(
        functools.partial(inward_kernel, pack),
        out_shape=jax.ShapeDtypeStruct(block_shape, jnp.bfloat16),
        in_specs=[pl.BlockSpec(memory_space=pltpu.SMEM), vmem, vmem],
        out_specs=vmem,
        scratch_shapes=[
            turned,
            pltpu.VMEM((lev_count,) + block_shape, jnp.bfloat16),
            pltpu.VMEM((lev_count,) + block_shape, jnp.bfloat16),
            pltpu.VMEM(block_shape, jnp.bfloat16),
            pltpu.VMEM(block_shape, jnp.bfloat16),
        ]
        + sems,
        compiler_params=pltpu.CompilerParams(collective_id=0, has_side_effects=True),
    )(pattern, spec_in, legendre)
    leaving = rows_step(fourier, circle_lengths, deal_list, mixing)
    product = pl.pallas_call(
        functools.partial(outward_kernel, pack, fields),
        out_shape=jax.ShapeDtypeStruct((slots, 2 * fields, local_cols), jnp.float32),
        in_specs=[
            pl.BlockSpec(memory_space=pltpu.SMEM),
            vmem,
            pl.BlockSpec(memory_space=pl.ANY),
        ],
        out_specs=vmem,
        scratch_shapes=[
            pltpu.VMEM(legendre.shape, jnp.bfloat16),
            pltpu.VMEM(block_shape, jnp.bfloat16),
            pltpu.VMEM((lev_count,) + block_shape, jnp.bfloat16),
            turned,
        ]
        + sems
        + [pltpu.SemaphoreType.DMA],
        compiler_params=pltpu.CompilerParams(collective_id=1, has_side_effects=True),
    )(pattern, leaving, legendre)
    return product.reshape(slots, 2, fields, local_cols)


def solution(mesh):
    return jax.shard_map(
        local,
        mesh=mesh,
        in_specs=(
            P("lat", None, None, "lev"),
            P("lat", "lev", None),
            P("lat", None, None),
            P(),
            P(),
            P(),
        ),
        out_specs=P("lat", None, None, "lev"),
        check_vma=False,
    )
```

```python
import functools
import math

import jax
import jax.numpy as jnp
from jax import lax
from jax.experimental import pallas as pl
from jax.experimental.pallas import tpu as pltpu
from jax.sharding import PartitionSpec as P

BLK = 128
SPAN = 2 * BLK
ACROSS = (((1,), (1,)), ((), ()))
STREAMS = 2
SPLIT = (3, 3)


def iota(shape, axis):
    return lax.broadcasted_iota(jnp.int32, shape, axis)


def unit(condition):
    return jnp.where(condition, 1.0, 0.0).astype(jnp.float32)


class Plan:
    def __init__(self, waves, fields, lat_count, lev_count, half_lat):
        self.waves, self.fields = waves, fields
        self.half_lat = half_lat
        self.devices = lat_count * lev_count
        self.rows = half_lat // self.devices
        self.hf = 2 * fields
        self.lanes = waves * 4 * fields
        self.share = max(
            n for n in range(1, self.rows + 1) if self.rows % n == 0 and (n == 1 or 4 * n * waves <= BLK)
        )
        self.groups = self.rows // self.share
        self.block = self.share * waves
        self.depth = 4 * self.block
        self.images = self.share * self.hf
        self.scale = (2.0 * waves) ** (-0.5)

    def tiles(self, group):
        last = ((group + 1) * self.share - 1) * self.devices + self.devices - 1
        return -(-(last + 6) // SPAN)

    def inside(self, group, tile):
        first = group * self.share * self.devices
        return (tile + 1) * SPAN - 1 < 3 + first - first // 2

    def chunks(self, pack):
        least = pack
        while least * self.devices % (pack * BLK) or least % self.share:
            least += pack
        units, out = self.rows // least, []
        first = self.rows
        for tenths in SPLIT:
            count = units * tenths // 10 * least
            if 0 < count < first:
                first -= count
                out.append((first, count))
        return out + [(0, first)]


def waves_at(deal, index, waves):
    out = jnp.zeros_like(index)
    for wave in range(waves):
        out = jnp.where(index == wave, deal[wave], out)
    return out


def fill_tables(plan, device, lengths, deal, table, row_length):
    wave = waves_at(deal, iota((plan.block, BLK), 0) % plan.waves, plan.waves).astype(jnp.float32)
    product = wave * iota((plan.block, BLK), 1).astype(jnp.float32)
    member = iota((plan.block, 1), 0) // plan.waves

    def fill(group, carry):
        length = jnp.zeros((plan.block, 1), jnp.float32)
        for each in range(plan.share):
            own = lengths[(group * plan.share + each) * plan.devices + device].astype(jnp.float32)
            length = jnp.where(member == each, own, length)
            row_length[pl.ds(group * plan.share + each, 1), :] = jnp.full((1, BLK), own, jnp.float32)
        turned = product - jnp.floor(product / length) * length
        angle = turned * (2.0 * math.pi) / length
        cosine, sine = jnp.cos(angle), jnp.sin(angle)
        last_cos, last_sin = cosine[:, BLK - 1 : BLK], sine[:, BLK - 1 : BLK]
        next_cos, next_sin = cosine[:, 1:2], sine[:, 1:2]
        table[group, 0] = cosine
        table[group, 1] = -sine
        table[group, 2] = jnp.broadcast_to(last_cos * next_cos - last_sin * next_sin, product.shape)
        table[group, 3] = jnp.broadcast_to(-last_sin * next_cos - last_cos * next_sin, product.shape)
        return carry

    lax.fori_loop(0, plan.groups, fill, 0)


def lane_waves(plan, deal):
    return waves_at(deal, iota((1, plan.lanes), 1) // (4 * plan.fields), plan.waves)


def live_rows(plan, device, deal):
    half_lat = plan.half_lat
    cut = lane_waves(plan, deal) * (half_lat // BLK) // (2 * half_lat)
    row = iota((plan.rows, 1), 0) * plan.devices + device
    return unit(row // BLK >= cut)


def image_sign(image, sine, odd):
    sign = jnp.ones(jnp.broadcast_shapes(sine.shape, odd.shape), jnp.float32)
    if image % 2:
        sign = sign * (1.0 - 2.0 * unit(sine))
    if image // 2:
        sign = sign * (1.0 - 2.0 * unit(odd))
    return sign


def fill_constants(plan, deal, mixing_ref, keep, gather, placed_sign, mixer, sum_sign, spread, fold_keep):
    waves, fields, hf, lanes = plan.waves, plan.fields, plan.hf, plan.lanes
    lane = iota((hf, lanes), 1)
    keep[...] = unit(lane // (2 * fields) % 2 * fields + lane % fields == iota((hf, lanes), 0))
    down, right = iota((2 * lanes, plan.depth), 0), iota((2 * lanes, plan.depth), 1)
    down_kind = down // lanes * 2 + down % lanes // fields % 2
    down_wave = down % lanes // (4 * fields)
    gather[...] = unit(
        (down_kind == right // plan.block) & (down_wave == right % waves)
    ).astype(jnp.bfloat16)
    right = iota((1, plan.depth), 1)
    mine = unit(iota((plan.images, 1), 0) // hf == right % plan.block // waves)
    odd = waves_at(deal, right % waves, waves) % 2 == 1
    sine = right // plan.block % 2 == 1
    for image in range(4):
        placed_sign[image] = mine * image_sign(image, sine, odd)
    pick = unit(iota((BLK, fields), 0) % fields == iota((BLK, fields), 1)).astype(jnp.bfloat16)
    half = lax.dot_general(
        pick, mixing_ref[...], ACROSS, preferred_element_type=jnp.float32
    ).astype(jnp.bfloat16)
    whole = lax.dot_general(half, pick, ACROSS, preferred_element_type=jnp.float32)
    same = iota((BLK, BLK), 0) // fields == iota((BLK, BLK), 1) // fields
    mixer[...] = jnp.where(same, whole, 0.0).astype(jnp.bfloat16)
    size, wide = sum_sign.shape
    down, right = iota((size, wide), 0), iota((size, wide), 1)
    odd = waves_at(deal, down % waves, waves) % 2 == 1
    sine = down // plan.block == 1
    sign = jnp.zeros((size, wide), jnp.float32)
    for image in range(4):
        sign = jnp.where(right // plan.images == image, image_sign(image, sine, odd), sign)
    sum_sign[...] = sign * unit(down % plan.block // waves == right % plan.images // hf)
    down, right = iota((2 * wide, lanes), 0), iota((2 * wide, lanes), 1)
    spread[...] = unit(
        down % hf == right // (2 * fields) % 2 * fields + right % fields
    ).astype(jnp.bfloat16)
    down, right = iota((size, lanes), 0), iota((size, lanes), 1)
    fold_keep[...] = unit(
        (down // plan.block == right // fields % 2) & (down % waves == right // (4 * fields))
    )


def fill_products(plan, device, row_length, deal, products, weights):
    length = jnp.concatenate([row_length[...]] * (plan.lanes // BLK), axis=1)
    wave = lane_waves(plan, deal).astype(jnp.float32)
    part = 1.0 - 2.0 * unit(iota((1, plan.lanes), 1) // plan.fields % 2 == 1)
    inverse, half = 1.0 / length, (0.5 * plan.scale) * length

    def whole(turns):
        return unit(turns == length * jnp.floor(turns * inverse + 0.5))

    for other in range(plan.waves):
        partner = rolled(plan, wave, other)
        products[other] = half * (whole(wave - partner) + part * whole(wave + partner))
    row = (iota((plan.rows, 1), 0) * plan.devices + device).astype(jnp.float32)
    weight = jnp.sin(math.pi * (row + 0.5) / (2 * plan.half_lat)) / jnp.sqrt(row_length[...])
    weights[0] = live_rows(plan, device, deal)
    weights[1] = weights[0] * jnp.concatenate([weight] * (plan.lanes // BLK), axis=1)


def rolled(plan, source, other):
    at = other * 4 * plan.fields
    return jnp.concatenate([source[:, at:], source[:, :at]], axis=1) if at else source


def place_coefficients(plan, first, values, keep, gather, placed_sign, mixer, left):
    rows = values.shape[0]
    narrow = values.astype(jnp.bfloat16)
    mixed = plan.scale * jnp.concatenate(
        [
            jnp.dot(narrow[:, at : at + BLK], mixer[...], preferred_element_type=jnp.float32)
            for at in range(0, plan.lanes, BLK)
        ],
        axis=1,
    )
    high = mixed.astype(jnp.bfloat16).astype(jnp.float32)
    spread = jnp.concatenate(
        [
            (source[:, None, :] * keep[...][None]).reshape(rows * plan.hf, plan.lanes).astype(jnp.bfloat16)
            for source in (high, mixed - high)
        ],
        axis=1,
    )
    placed = jnp.dot(spread, gather[...], preferred_element_type=jnp.float32)
    for group in range(rows // plan.share):
        own = placed[group * plan.images : (group + 1) * plan.images]
        for image in range(4):
            left[
                first // plan.share + group, image * plan.images : (image + 1) * plan.images, :
            ] = (own * placed_sign[image]).astype(jnp.bfloat16)


def walk_circles(plan, groups, device, lengths, table, left, total):
    position = iota((1, SPAN), 1)
    member = iota((plan.block, 1), 0) // plan.waves

    def phases(group, tile, cos_now, sin_now):
        step_cos, step_sin = table[group, 2], table[group, 3]
        cosines, sines = [], []
        for _ in range(SPAN // BLK):
            cosines.append(cos_now)
            sines.append(sin_now)
            cos_now, sin_now = (
                cos_now * step_cos - sin_now * step_sin,
                sin_now * step_cos + cos_now * step_sin,
            )
        cosine, sine = jnp.concatenate(cosines, axis=1), jnp.concatenate(sines, axis=1)
        near, far = cosine.astype(jnp.bfloat16), sine.astype(jnp.bfloat16)
        weights = jnp.concatenate([near, far, near, far], axis=0)
        if tile > 0 and plan.inside(group, tile):
            return cos_now, sin_now, weights, weights[: 2 * plan.block]
        at = position + tile * SPAN
        quarter = jnp.zeros((plan.block, 1), jnp.int32)
        for each in range(plan.share):
            own = lengths[(group * plan.share + each) * plan.devices + device]
            quarter = jnp.where(member == each, lax.shift_right_logical(own, 2), quarter)
        share = jnp.where(at < quarter, 1.0, jnp.where(at == quarter, 0.5, 0.0)).astype(jnp.float32)
        if tile == 0:
            share = share * jnp.where(at == 0, 0.5, 1.0).astype(jnp.float32)
        shared = jnp.concatenate([cosine * share, sine * share], axis=0).astype(jnp.bfloat16)
        return cos_now, sin_now, weights, shared

    streams = [[] for _ in range(STREAMS)]
    for group in sorted(groups, key=lambda group: -plan.tiles(group)):
        min(streams, key=len).extend((group, tile) for tile in range(plan.tiles(group)))
    state, sums, waiting = {}, {}, []

    def finish():
        for group, shared, grid in waiting:
            extra = lax.dot_general(
                shared,
                jnp.tanh(grid).astype(jnp.bfloat16),
                ACROSS,
                preferred_element_type=jnp.float32,
            )
            sums[group] = sums[group] + extra if group in sums else extra
        waiting.clear()

    for step in range(max(len(stream) for stream in streams)):
        started = []
        for stream in streams:
            if step < len(stream):
                group, tile = stream[step]
                if group not in state:
                    state[group] = table[group, 0], table[group, 1]
                cos_now, sin_now, weights, shared = phases(group, tile, *state[group])
                state[group] = cos_now, sin_now
                grid = jnp.dot(left[group], weights, preferred_element_type=jnp.float32)
                started.append((group, shared, grid))
        finish()
        waiting.extend(started)
    finish()
    size = 2 * plan.block
    for group in groups:
        total[group * size : (group + 1) * size, :] = sums[group]


def fold_circles(plan, sums, sum_sign, spread, fold_keep):
    size, wide = sum_sign.shape
    count = sums.shape[0] // size
    signed = (sums.reshape(count, size, wide) * sum_sign[...][None]).reshape(count * size, wide)
    high = signed.astype(jnp.bfloat16)
    low = (signed - high.astype(jnp.float32)).astype(jnp.bfloat16)
    folded = jnp.dot(
        jnp.concatenate([high, low], axis=1), spread[...], preferred_element_type=jnp.float32
    )
    kept = (folded.reshape(count, size, plan.lanes) * fold_keep[...][None]).reshape(
        count, 2, plan.share, plan.waves, plan.lanes
    )
    return jnp.sum(jnp.sum(kept, axis=1), axis=2).reshape(count * plan.share, plan.lanes)


def column_masks(plan, deal, slots, local_cols):
    column = iota((1, local_cols), 1) + lax.axis_index("lev") * local_cols
    odd = (1 - 2 * (column % 2)).astype(jnp.float32)
    masks = []
    for slot in range(slots):
        wave = deal[lax.axis_index("lat") * slots + slot]
        masks.append(unit(column // BLK * BLK <= plan.half_lat - 1 - wave))
    return odd, masks


def peers_of(axis):
    count = lax.axis_size(axis)
    return [lax.rem(lax.axis_index(axis) + off, count) for off in range(1, count)]


def expect(total):
    pl.semaphore_wait(pltpu.get_barrier_semaphore(), total)


def hail():
    barrier = pltpu.get_barrier_semaphore()
    total = 0
    for axis in ("lat", "lev"):
        for peer in peers_of(axis):
            pl.semaphore_signal(
                barrier, inc=1, device_id={axis: peer}, device_id_type=pl.DeviceIdType.MESH
            )
            total += 1
    return total


def send(axis, sources, target, sems):
    copies = []
    for step, peer in enumerate(peers_of(axis)):
        copy = pltpu.make_async_remote_copy(
            src_ref=sources(peer),
            dst_ref=target,
            send_sem=sems.at[0, step],
            recv_sem=sems.at[1, step],
            device_id={axis: peer},
            device_id_type=pl.DeviceIdType.MESH,
        )
        copy.start()
        copies.append(copy)
    return copies


def arrivals(axis, copies):
    count, index = lax.axis_size(axis), lax.axis_index(axis)
    for off, copy in enumerate(copies, 1):
        copy.wait_recv()
        yield lax.rem(index + count - off, count)


def chunk_scratch(count, pack, width, lat_count, lev_count):
    block = (lat_count, count // pack, width)
    devices = lat_count * lev_count
    return [
        pltpu.VMEM((lev_count,) + block, jnp.bfloat16),
        pltpu.VMEM((lev_count,) + block, jnp.bfloat16),
        pltpu.VMEM(block, jnp.bfloat16),
        pltpu.VMEM(block, jnp.bfloat16),
        pltpu.VMEM(block, jnp.bfloat16),
        pltpu.VMEM(block, jnp.bfloat16),
        pltpu.VMEM((lev_count,) + block, jnp.bfloat16),
        pltpu.VMEM((width // BLK, count // pack * devices, BLK), jnp.float32),
        pltpu.SemaphoreType.DMA((2, 2, lev_count)),
        pltpu.SemaphoreType.DMA((2, 2, lat_count)),
    ]


CHUNK_REFS = 10


def round_trip_kernel(plan, pack, chunks, lengths, deal, spec_ref, legendre_ref, mixing_ref, out_ref, *scratch):
    held, load_sems, left, table, total, row_length, products, weights, values_ref = scratch[:9]
    keep, gather, placed_sign, mixer, sum_sign, spread, fold_keep = scratch[9:16]
    buffers = [
        scratch[16 + at * CHUNK_REFS : 16 + (at + 1) * CHUNK_REFS] for at in range(len(chunks))
    ]
    slots, local_cols, half_lat = held.shape
    fields, devices = plan.fields, plan.devices
    lat_count, lev_count = lax.axis_size("lat"), lax.axis_size("lev")
    lev_index, lat_index = lax.axis_index("lev"), lax.axis_index("lat")
    device = lev_index * lat_count + lat_index
    part_width = 4 * fields
    part_span = slots * part_width
    width = part_span * pack
    faces = width // BLK
    loads = []
    for at, (first, count) in enumerate(chunks):
        columns = pl.ds(first * devices, count * devices)
        load = pltpu.make_async_copy(
            legendre_ref.at[:, :, columns], held.at[:, :, columns], load_sems.at[at]
        )
        load.start()
        loads.append(load)
    greetings = hail()
    odd, masks = column_masks(plan, deal, slots, local_cols)
    lefts = []
    for slot in range(slots):
        kept = jnp.concatenate([spec_ref[slot, 0], spec_ref[slot, 1]], axis=0).astype(jnp.float32)
        kept = kept * masks[slot]
        lefts.append(jnp.concatenate([kept, kept * odd], axis=0).astype(jnp.bfloat16))

    sent = []
    for at, (first, count) in enumerate(chunks):
        leaving, arriving, turned, lev_sems = (buffers[at][n] for n in (0, 1, 7, 8))
        each = count // pack
        loads[at].wait()
        sums = [
            jnp.dot(
                lefts[slot],
                held[slot, :, first * devices : (first + count) * devices],
                preferred_element_type=jnp.float32,
            )
            for slot in range(slots)
        ]
        for block in range(each * devices // BLK):
            piece = jnp.concatenate(
                [
                    value[:, part * each * devices + block * BLK : part * each * devices + (block + 1) * BLK]
                    for part in range(pack)
                    for value in sums
                ],
                axis=0,
            )
            for face in range(faces):
                turned[face, block * BLK : (block + 1) * BLK, :] = piece[face * BLK : (face + 1) * BLK].T
        for target in range(devices):
            for face in range(faces):
                leaving[target // lat_count, target % lat_count, :, face * BLK : (face + 1) * BLK] = (
                    turned[face, pl.ds(target, each, stride=devices), :].astype(jnp.bfloat16)
                )
        if at == 0:
            expect(greetings)
        sent.append(send("lev", lambda peer, leaving=leaving: leaving.at[peer], arriving.at[lev_index], lev_sems.at[0]))
    finished = list(sent)

    fill_constants(plan, deal, mixing_ref, keep, gather, placed_sign, mixer, sum_sign, spread, fold_keep)
    fill_tables(plan, device, lengths, deal, table, row_length)

    crossed = []
    for at, (first, count) in enumerate(chunks):
        arriving, summed, landed, turned, lat_sems = (buffers[at][n] for n in (1, 2, 3, 7, 9))
        each = count // pack
        sum_of = jnp.stack(
            [
                jnp.concatenate(
                    [
                        turned[face, pl.ds(lev_index * lat_count + side, each, stride=devices), :]
                        for face in range(faces)
                    ],
                    axis=1,
                )
                for side in range(lat_count)
            ]
        )
        for peer in arrivals("lev", sent[at]):
            sum_of = sum_of + arriving[peer].astype(jnp.float32)
        summed[...] = sum_of.astype(jnp.bfloat16)
        crossed.append(
            send("lat", lambda peer, summed=summed: summed.at[peer], landed.at[lat_index], lat_sems.at[0])
        )
        landed[lat_index] = summed[lat_index]
        if at == 0:
            fill_products(plan, device, row_length, deal, products, weights)
    finished += crossed

    returned, shared = [], []

    def pass_on(at):
        back, gathered, lev_sems = (buffers[at][n] for n in (5, 6, 8))
        for _ in arrivals("lat", returned[at]):
            pass
        copies = send("lev", lambda peer: back, gathered.at[lev_index], lev_sems.at[1])
        gathered[lev_index] = back[...]
        shared.append(copies)
        finished.append(copies)

    for at, (first, count) in enumerate(chunks):
        landed, leaving_rows, back, lat_sems = (buffers[at][n] for n in (3, 4, 5, 9))
        each = count // pack
        for _ in arrivals("lat", crossed[at]):
            pass
        blocks = [landed[side].astype(jnp.float32) for side in range(lat_count)]
        values = jnp.concatenate(
            [
                jnp.concatenate(
                    [block[:, part * part_span : (part + 1) * part_span] for block in blocks], axis=1
                )
                for part in range(pack)
            ],
            axis=0,
        )
        values = values * weights[0, first : first + count]
        values_ref[first : first + count] = values
        place_coefficients(plan, first, values, keep, gather, placed_sign, mixer, left)
        groups = list(range(first // plan.share, (first + count) // plan.share))
        if at:
            middle = len(groups) // 2
            walk_circles(plan, groups[middle:], device, lengths, table, left, total)
            pass_on(at - 1)
            groups = groups[:middle]
        if groups:
            walk_circles(plan, groups, device, lengths, table, left, total)
        size = 2 * plan.block
        result = fold_circles(
            plan,
            total[first // plan.share * size : (first + count) // plan.share * size, :],
            sum_sign,
            spread,
            fold_keep,
        )
        values = values_ref[first : first + count]
        for other in range(plan.waves):
            result = result + products[other, first : first + count] * rolled(plan, values, other)
        result = result * weights[1, first : first + count]
        for side in range(lat_count):
            leaving_rows[side] = jnp.concatenate(
                [
                    result[part * each : (part + 1) * each, side * part_span : (side + 1) * part_span]
                    for part in range(pack)
                ],
                axis=1,
            ).astype(jnp.bfloat16)
        returned.append(
            send("lat", lambda peer, rows=leaving_rows: rows.at[peer], back.at[lat_index], lat_sems.at[1])
        )
        back[lat_index] = leaving_rows[lat_index]
    finished += returned

    sums = [None] * slots
    for at, (first, count) in enumerate(chunks):
        gathered, turned = buffers[at][6], buffers[at][7]
        each = count // pack
        if at == len(chunks) - 1:
            pass_on(at)
        for _ in arrivals("lev", shared[at]):
            pass
        for source in range(devices):
            block = gathered[source // lat_count, source % lat_count].astype(jnp.float32)
            for face in range(faces):
                turned[face, pl.ds(source, each, stride=devices), :] = block[:, face * BLK : (face + 1) * BLK]
        sides = [turned[face].astype(jnp.bfloat16) for face in range(faces)]
        for slot in range(slots):
            for part in range(pack):
                lane = part * part_span + slot * part_width
                start = (first + part * each) * devices
                value = jnp.dot(
                    held[slot, :, start : start + each * devices],
                    sides[lane // BLK],
                    preferred_element_type=jnp.float32,
                )[:, lane % BLK : lane % BLK + part_width]
                sums[slot] = value if sums[slot] is None else sums[slot] + value
    odd, masks = column_masks(plan, deal, slots, local_cols)
    for slot in range(slots):
        flat = sums[slot].T
        out_ref[slot] = (flat[: 2 * fields] + odd * flat[2 * fields :]) * masks[slot]
    for copies in finished:
        for copy in copies:
            copy.wait_send()


def local(spec_in, legendre, pattern, deal_list, circle_lengths, mixing):
    lat_count, lev_count = lax.axis_size("lat"), lax.axis_size("lev")
    slots, local_cols, half_lat = legendre.shape
    fields, waves = spec_in.shape[2], deal_list.shape[0]
    plan = Plan(waves, fields, lat_count, lev_count, half_lat)
    span = 4 * slots * fields
    pack = max(1, BLK // span)
    chunks = plan.chunks(pack)
    vmem = pl.BlockSpec(memory_space=pltpu.VMEM)
    smem = pl.BlockSpec(memory_space=pltpu.SMEM)
    size, wide = 2 * plan.block, 4 * plan.images
    scratch = [
        pltpu.VMEM(legendre.shape, jnp.bfloat16),
        pltpu.SemaphoreType.DMA((len(chunks),)),
        pltpu.VMEM((plan.groups, wide, plan.depth), jnp.bfloat16),
        pltpu.VMEM((plan.groups, 4, plan.block, BLK), jnp.float32),
        pltpu.VMEM((plan.groups * size, wide), jnp.float32),
        pltpu.VMEM((plan.rows, BLK), jnp.float32),
        pltpu.VMEM((waves, plan.rows, plan.lanes), jnp.float32),
        pltpu.VMEM((2, plan.rows, plan.lanes), jnp.float32),
        pltpu.VMEM((plan.rows, plan.lanes), jnp.float32),
        pltpu.VMEM((plan.hf, plan.lanes), jnp.float32),
        pltpu.VMEM((2 * plan.lanes, plan.depth), jnp.bfloat16),
        pltpu.VMEM((4, plan.images, plan.depth), jnp.float32),
        pltpu.VMEM((BLK, BLK), jnp.bfloat16),
        pltpu.VMEM((size, wide), jnp.float32),
        pltpu.VMEM((2 * wide, plan.lanes), jnp.bfloat16),
        pltpu.VMEM((size, plan.lanes), jnp.float32),
    ]
    for _, count in chunks:
        scratch += chunk_scratch(count, pack, span * pack, lat_count, lev_count)
    product = pl.pallas_call(
        functools.partial(round_trip_kernel, plan, pack, chunks),
        out_shape=jax.ShapeDtypeStruct((slots, 2 * fields, local_cols), jnp.float32),
        in_specs=[smem, smem, vmem, pl.BlockSpec(memory_space=pl.ANY), vmem],
        out_specs=vmem,
        scratch_shapes=scratch,
        compiler_params=pltpu.CompilerParams(collective_id=0, has_side_effects=True),
    )(circle_lengths, deal_list, spec_in, legendre, mixing)
    return product.reshape(slots, 2, fields, local_cols)


def solution(mesh):
    return jax.shard_map(
        local,
        mesh=mesh,
        in_specs=(
            P("lat", None, None, "lev"),
            P("lat", "lev", None),
            P("lat", None, None),
            P(),
            P(),
            P(),
        ),
        out_specs=P("lat", None, None, "lev"),
        check_vma=False,
    )
```

```python
import functools
import math

import jax
import jax.numpy as jnp
from jax import lax
from jax.experimental import pallas as pl
from jax.experimental.pallas import tpu as pltpu
from jax.sharding import PartitionSpec as P

BLK = 128
SPAN = 2 * BLK
ACROSS = (((1,), (1,)), ((), ()))
STREAMS = 2
SPLIT = ((8, 10), (0, 6), (6, 8))
DIRECT = 64


def iota(shape, axis):
    return lax.broadcasted_iota(jnp.int32, shape, axis)


def unit(condition):
    return jnp.where(condition, 1.0, 0.0).astype(jnp.float32)


class Plan:
    def __init__(self, waves, fields, lat_count, lev_count, half_lat):
        self.waves, self.fields = waves, fields
        self.half_lat = half_lat
        self.devices = lat_count * lev_count
        self.rows = half_lat // self.devices
        self.hf = 2 * fields
        self.lanes = waves * 4 * fields
        self.share = max(
            n for n in range(1, self.rows + 1) if self.rows % n == 0 and (n == 1 or 4 * n * waves <= BLK)
        )
        self.groups = self.rows // self.share
        self.block = self.share * waves
        self.depth = 4 * self.block
        self.images = self.share * self.hf
        self.scale = (2.0 * waves) ** (-0.5)

    def tiles(self, group):
        last = ((group + 1) * self.share - 1) * self.devices + self.devices - 1
        return -(-(last + 6) // SPAN)

    def inside(self, group, tile):
        first = group * self.share * self.devices
        return (tile + 1) * SPAN - 1 < 3 + first - first // 2

    def chunks(self, pack):
        least = pack
        while least * self.devices % (pack * BLK) or least % self.share:
            least += pack
        units = self.rows // least
        marks = [(units * start // 10 * least, units * stop // 10 * least) for start, stop in SPLIT]
        return [(start, stop - start) for start, stop in marks if stop > start]


def waves_at(deal, index, waves):
    out = jnp.zeros_like(index)
    for wave in range(waves):
        out = jnp.where(index == wave, deal[wave], out)
    return out


def fill_tables(plan, device, lengths, deal, table, row_length):
    wave = waves_at(deal, iota((plan.block, BLK), 0) % plan.waves, plan.waves).astype(jnp.float32)
    product = wave * iota((plan.block, BLK), 1).astype(jnp.float32)
    member = iota((plan.block, 1), 0) // plan.waves

    def fill(group, carry):
        length = jnp.zeros((plan.block, 1), jnp.float32)
        for each in range(plan.share):
            own = lengths[(group * plan.share + each) * plan.devices + device].astype(jnp.float32)
            length = jnp.where(member == each, own, length)
            row_length[pl.ds(group * plan.share + each, 1), :] = jnp.full((1, BLK), own, jnp.float32)
        turned = product - jnp.floor(product / length) * length
        angle = turned * (2.0 * math.pi) / length
        cosine, sine = jnp.cos(angle), jnp.sin(angle)
        last_cos, last_sin = cosine[:, BLK - 1 : BLK], sine[:, BLK - 1 : BLK]
        next_cos, next_sin = cosine[:, 1:2], sine[:, 1:2]
        table[group, 0] = cosine
        table[group, 1] = -sine
        table[group, 2] = jnp.broadcast_to(last_cos * next_cos - last_sin * next_sin, product.shape)
        table[group, 3] = jnp.broadcast_to(-last_sin * next_cos - last_cos * next_sin, product.shape)
        return carry

    lax.fori_loop(0, plan.groups, fill, 0)


def lane_waves(plan, deal):
    return waves_at(deal, iota((1, plan.lanes), 1) // (4 * plan.fields), plan.waves)


def live_rows(plan, device, deal):
    half_lat = plan.half_lat
    cut = lane_waves(plan, deal) * (half_lat // BLK) // (2 * half_lat)
    row = iota((plan.rows, 1), 0) * plan.devices + device
    return unit(row // BLK >= cut)


def image_sign(image, sine, odd):
    sign = jnp.ones(jnp.broadcast_shapes(sine.shape, odd.shape), jnp.float32)
    if image % 2:
        sign = sign * (1.0 - 2.0 * unit(sine))
    if image // 2:
        sign = sign * (1.0 - 2.0 * unit(odd))
    return sign


def fill_constants(plan, deal, mixing_ref, keep, gather, placed_sign, mixer, sum_sign, spread, fold_keep):
    waves, fields, hf, lanes = plan.waves, plan.fields, plan.hf, plan.lanes
    lane = iota((hf, lanes), 1)
    keep[...] = unit(lane // (2 * fields) % 2 * fields + lane % fields == iota((hf, lanes), 0))
    down, right = iota((2 * lanes, plan.depth), 0), iota((2 * lanes, plan.depth), 1)
    down_kind = down // lanes * 2 + down % lanes // fields % 2
    down_wave = down % lanes // (4 * fields)
    gather[...] = unit(
        (down_kind == right // plan.block) & (down_wave == right % waves)
    ).astype(jnp.bfloat16)
    right = iota((1, plan.depth), 1)
    mine = unit(iota((plan.images, 1), 0) // hf == right % plan.block // waves)
    odd = waves_at(deal, right % waves, waves) % 2 == 1
    sine = right // plan.block % 2 == 1
    for image in range(4):
        placed_sign[image] = mine * image_sign(image, sine, odd)
    pick = unit(iota((BLK, fields), 0) % fields == iota((BLK, fields), 1)).astype(jnp.bfloat16)
    half = lax.dot_general(
        pick, mixing_ref[...], ACROSS, preferred_element_type=jnp.float32
    ).astype(jnp.bfloat16)
    whole = lax.dot_general(half, pick, ACROSS, preferred_element_type=jnp.float32)
    same = iota((BLK, BLK), 0) // fields == iota((BLK, BLK), 1) // fields
    mixer[...] = jnp.where(same, whole, 0.0).astype(jnp.bfloat16)
    size, wide = sum_sign.shape
    down, right = iota((size, wide), 0), iota((size, wide), 1)
    odd = waves_at(deal, down % waves, waves) % 2 == 1
    sine = down // plan.block == 1
    sign = jnp.zeros((size, wide), jnp.float32)
    for image in range(4):
        sign = jnp.where(right // plan.images == image, image_sign(image, sine, odd), sign)
    sum_sign[...] = sign * unit(down % plan.block // waves == right % plan.images // hf)
    down, right = iota((2 * wide, lanes), 0), iota((2 * wide, lanes), 1)
    spread[...] = unit(
        down % hf == right // (2 * fields) % 2 * fields + right % fields
    ).astype(jnp.bfloat16)
    down, right = iota((size, lanes), 0), iota((size, lanes), 1)
    fold_keep[...] = unit(
        (down // plan.block == right // fields % 2) & (down % waves == right // (4 * fields))
    )


def fill_products(plan, device, row_length, deal, products, weights):
    length = jnp.concatenate([row_length[...]] * (plan.lanes // BLK), axis=1)
    wave = lane_waves(plan, deal).astype(jnp.float32)
    part = 1.0 - 2.0 * unit(iota((1, plan.lanes), 1) // plan.fields % 2 == 1)
    inverse, half = 1.0 / length, (0.5 * plan.scale) * length

    def whole(turns):
        return unit(turns == length * jnp.floor(turns * inverse + 0.5))

    for other in range(plan.waves):
        partner = rolled(plan, wave, other)
        products[other] = half * (whole(wave - partner) + part * whole(wave + partner))
    row = (iota((plan.rows, 1), 0) * plan.devices + device).astype(jnp.float32)
    weight = jnp.sin(math.pi * (row + 0.5) / (2 * plan.half_lat)) / jnp.sqrt(row_length[...])
    weights[0] = live_rows(plan, device, deal)
    weights[1] = weights[0] * jnp.concatenate([weight] * (plan.lanes // BLK), axis=1)


def rolled(plan, source, other):
    at = other * 4 * plan.fields
    return jnp.concatenate([source[:, at:], source[:, :at]], axis=1) if at else source


def place_coefficients(plan, first, values, keep, gather, placed_sign, mixer, left):
    rows = values.shape[0]
    narrow = values.astype(jnp.bfloat16)
    mixed = plan.scale * jnp.concatenate(
        [
            jnp.dot(narrow[:, at : at + BLK], mixer[...], preferred_element_type=jnp.float32)
            for at in range(0, plan.lanes, BLK)
        ],
        axis=1,
    )
    high = mixed.astype(jnp.bfloat16).astype(jnp.float32)
    spread = jnp.concatenate(
        [
            (source[:, None, :] * keep[...][None]).reshape(rows * plan.hf, plan.lanes).astype(jnp.bfloat16)
            for source in (high, mixed - high)
        ],
        axis=1,
    )
    placed = jnp.dot(spread, gather[...], preferred_element_type=jnp.float32)
    for group in range(rows // plan.share):
        own = placed[group * plan.images : (group + 1) * plan.images]
        for image in range(4):
            left[
                first // plan.share + group, image * plan.images : (image + 1) * plan.images, :
            ] = (own * placed_sign[image]).astype(jnp.bfloat16)


def walk_circles(plan, groups, device, lengths, table, left, total):
    position = iota((1, SPAN), 1)
    member = iota((plan.block, 1), 0) // plan.waves

    def phases(group, tile, cos_now, sin_now):
        step_cos, step_sin = table[group, 2], table[group, 3]
        cosines, sines = [], []
        for _ in range(SPAN // BLK):
            cosines.append(cos_now)
            sines.append(sin_now)
            cos_now, sin_now = (
                cos_now * step_cos - sin_now * step_sin,
                sin_now * step_cos + cos_now * step_sin,
            )
        cosine, sine = jnp.concatenate(cosines, axis=1), jnp.concatenate(sines, axis=1)
        near, far = cosine.astype(jnp.bfloat16), sine.astype(jnp.bfloat16)
        weights = jnp.concatenate([near, far, near, far], axis=0)
        if tile > 0 and plan.inside(group, tile):
            return cos_now, sin_now, weights, weights[: 2 * plan.block]
        at = position + tile * SPAN
        quarter = jnp.zeros((plan.block, 1), jnp.int32)
        for each in range(plan.share):
            own = lengths[(group * plan.share + each) * plan.devices + device]
            quarter = jnp.where(member == each, lax.shift_right_logical(own, 2), quarter)
        share = jnp.where(at < quarter, 1.0, jnp.where(at == quarter, 0.5, 0.0)).astype(jnp.float32)
        if tile == 0:
            share = share * jnp.where(at == 0, 0.5, 1.0).astype(jnp.float32)
        shared = jnp.concatenate([cosine * share, sine * share], axis=0).astype(jnp.bfloat16)
        return cos_now, sin_now, weights, shared

    streams = [[] for _ in range(STREAMS)]
    for group in sorted(groups, key=lambda group: -plan.tiles(group)):
        min(streams, key=len).extend((group, tile) for tile in range(plan.tiles(group)))
    state, sums, waiting = {}, {}, []

    def finish():
        for group, shared, grid in waiting:
            extra = lax.dot_general(
                shared,
                jnp.tanh(grid).astype(jnp.bfloat16),
                ACROSS,
                preferred_element_type=jnp.float32,
            )
            sums[group] = sums[group] + extra if group in sums else extra
        waiting.clear()

    for step in range(max(len(stream) for stream in streams)):
        started = []
        for stream in streams:
            if step < len(stream):
                group, tile = stream[step]
                if group not in state:
                    state[group] = table[group, 0], table[group, 1]
                cos_now, sin_now, weights, shared = phases(group, tile, *state[group])
                state[group] = cos_now, sin_now
                grid = jnp.dot(left[group], weights, preferred_element_type=jnp.float32)
                started.append((group, shared, grid))
        finish()
        waiting.extend(started)
    finish()
    size = 2 * plan.block
    for group in groups:
        total[group * size : (group + 1) * size, :] = sums[group]


def fold_circles(plan, sums, sum_sign, spread, fold_keep):
    size, wide = sum_sign.shape
    count = sums.shape[0] // size
    signed = (sums.reshape(count, size, wide) * sum_sign[...][None]).reshape(count * size, wide)
    high = signed.astype(jnp.bfloat16)
    low = (signed - high.astype(jnp.float32)).astype(jnp.bfloat16)
    folded = jnp.dot(
        jnp.concatenate([high, low], axis=1), spread[...], preferred_element_type=jnp.float32
    )
    kept = (folded.reshape(count, size, plan.lanes) * fold_keep[...][None]).reshape(
        count, 2, plan.share, plan.waves, plan.lanes
    )
    return jnp.sum(jnp.sum(kept, axis=1), axis=2).reshape(count * plan.share, plan.lanes)


def column_masks(plan, deal, slots, local_cols):
    column = iota((1, local_cols), 1) + lax.axis_index("lev") * local_cols
    odd = (1 - 2 * (column % 2)).astype(jnp.float32)
    masks = []
    for slot in range(slots):
        wave = deal[lax.axis_index("lat") * slots + slot]
        masks.append(unit(column // BLK * BLK <= plan.half_lat - 1 - wave))
    return odd, masks


def peers_of(axis):
    count = lax.axis_size(axis)
    return [lax.rem(lax.axis_index(axis) + off, count) for off in range(1, count)]


def expect(total):
    pl.semaphore_wait(pltpu.get_barrier_semaphore(), total)


def others(count):
    lat_count = lax.axis_size("lat")
    me = lax.axis_index("lev") * lat_count + lax.axis_index("lat")
    for off in range(1, count):
        peer = lax.rem(me + off, count)
        yield {"lat": lax.rem(peer, lat_count), "lev": lax.div(peer, lat_count)}


def hail(direct):
    barrier = pltpu.get_barrier_semaphore()
    if direct:
        peers = list(others(lax.axis_size("lat") * lax.axis_size("lev")))
    else:
        peers = [{axis: peer} for axis in ("lat", "lev") for peer in peers_of(axis)]
    for peer in peers:
        pl.semaphore_signal(barrier, inc=1, device_id=peer, device_id_type=pl.DeviceIdType.MESH)
    return len(peers)


def send_all(sources, target, sems):
    copies = []
    for step, peer in enumerate(others(lax.axis_size("lat") * lax.axis_size("lev"))):
        copy = pltpu.make_async_remote_copy(
            src_ref=sources(peer["lev"], peer["lat"]),
            dst_ref=target,
            send_sem=sems.at[0, step],
            recv_sem=sems.at[1, step],
            device_id=peer,
            device_id_type=pl.DeviceIdType.MESH,
        )
        copy.start()
        copies.append(copy)
    return copies


def send(axis, sources, target, sems):
    copies = []
    for step, peer in enumerate(peers_of(axis)):
        copy = pltpu.make_async_remote_copy(
            src_ref=sources(peer),
            dst_ref=target,
            send_sem=sems.at[0, step],
            recv_sem=sems.at[1, step],
            device_id={axis: peer},
            device_id_type=pl.DeviceIdType.MESH,
        )
        copy.start()
        copies.append(copy)
    return copies


def arrivals(axis, copies):
    count, index = lax.axis_size(axis), lax.axis_index(axis)
    for off, copy in enumerate(copies, 1):
        copy.wait_recv()
        yield lax.rem(index + count - off, count)


def chunk_scratch(count, pack, width, lat_count, lev_count):
    block = (lat_count, count // pack, width)
    devices = lat_count * lev_count
    return [
        pltpu.VMEM((lev_count,) + block, jnp.bfloat16),
        pltpu.VMEM((lev_count,) + block, jnp.bfloat16),
        pltpu.VMEM(block, jnp.bfloat16),
        pltpu.VMEM(block, jnp.bfloat16),
        pltpu.VMEM(block, jnp.bfloat16),
        pltpu.VMEM(block, jnp.bfloat16),
        pltpu.VMEM((lev_count,) + block, jnp.bfloat16),
        pltpu.VMEM((width // BLK, count // pack * devices, BLK), jnp.float32),
        pltpu.SemaphoreType.DMA((2, 2, lev_count)),
        pltpu.SemaphoreType.DMA((2, 2, lat_count)),
    ]


CHUNK_REFS = 10


def round_trip_kernel(plan, pack, chunks, lengths, deal, spec_ref, legendre_ref, mixing_ref, out_ref, *scratch):
    held, load_sems, left, table, total, row_length, products, weights, values_ref = scratch[:9]
    keep, gather, placed_sign, mixer, sum_sign, spread, fold_keep, direct_sems = scratch[9:17]
    buffers = [
        scratch[17 + at * CHUNK_REFS : 17 + (at + 1) * CHUNK_REFS] for at in range(len(chunks))
    ]
    slots, local_cols, half_lat = held.shape
    fields, devices = plan.fields, plan.devices
    lat_count, lev_count = lax.axis_size("lat"), lax.axis_size("lev")
    lev_index, lat_index = lax.axis_index("lev"), lax.axis_index("lat")
    device = lev_index * lat_count + lat_index
    part_width = 4 * fields
    part_span = slots * part_width
    width = part_span * pack
    faces = width // BLK
    last = len(chunks) - 1
    direct = devices <= DIRECT
    loads = []
    for at, (first, count) in enumerate(chunks):
        columns = pl.ds(first * devices, count * devices)
        load = pltpu.make_async_copy(
            legendre_ref.at[:, :, columns], held.at[:, :, columns], load_sems.at[at]
        )
        load.start()
        loads.append(load)
    greetings = hail(direct)
    odd, masks = column_masks(plan, deal, slots, local_cols)
    lefts = []
    for slot in range(slots):
        kept = jnp.concatenate([spec_ref[slot, 0], spec_ref[slot, 1]], axis=0).astype(jnp.float32)
        kept = kept * masks[slot]
        lefts.append(jnp.concatenate([kept, kept * odd], axis=0).astype(jnp.bfloat16))

    finished = []
    reduced, crossed, returned, shared = {}, {}, {}, {}

    def project(at):
        first, count = chunks[at]
        leaving, turned = buffers[at][0], buffers[at][7]
        each = count // pack
        loads[at].wait()
        sums = [
            jnp.dot(
                lefts[slot],
                held[slot, :, first * devices : (first + count) * devices],
                preferred_element_type=jnp.float32,
            )
            for slot in range(slots)
        ]
        for block in range(each * devices // BLK):
            piece = jnp.concatenate(
                [
                    value[:, part * each * devices + block * BLK : part * each * devices + (block + 1) * BLK]
                    for part in range(pack)
                    for value in sums
                ],
                axis=0,
            )
            for face in range(faces):
                turned[face, block * BLK : (block + 1) * BLK, :] = piece[face * BLK : (face + 1) * BLK].T
        for target in range(devices):
            for face in range(faces):
                leaving[target // lat_count, target % lat_count, :, face * BLK : (face + 1) * BLK] = (
                    turned[face, pl.ds(target, each, stride=devices), :].astype(jnp.bfloat16)
                )

    def start_reduce(at):
        leaving, arriving, lev_sems = (buffers[at][n] for n in (0, 1, 8))
        if at == 0 and direct:
            copies = send_all(
                lambda lev, lat: leaving.at[lev, lat], arriving.at[lev_index, lat_index], direct_sems.at[0]
            )
            arriving[lev_index, lat_index] = leaving[lev_index, lat_index]
        else:
            copies = send("lev", lambda peer: leaving.at[peer], arriving.at[lev_index], lev_sems.at[0])
        reduced[at] = copies
        finished.append(copies)

    def start_cross(at):
        count = chunks[at][1]
        arriving, summed, landed, turned, lat_sems = (buffers[at][n] for n in (1, 2, 3, 7, 9))
        each = count // pack
        total_of = jnp.stack(
            [
                jnp.concatenate(
                    [
                        turned[face, pl.ds(lev_index * lat_count + side, each, stride=devices), :]
                        for face in range(faces)
                    ],
                    axis=1,
                )
                for side in range(lat_count)
            ]
        )
        for peer in arrivals("lev", reduced[at]):
            total_of = total_of + arriving[peer].astype(jnp.float32)
        summed[...] = total_of.astype(jnp.bfloat16)
        crossed[at] = send("lat", lambda peer: summed.at[peer], landed.at[lat_index], lat_sems.at[0])
        landed[lat_index] = summed[lat_index]
        finished.append(crossed[at])

    def land(at):
        arriving, landed = buffers[at][1], buffers[at][3]
        if at == 0 and direct:
            for copy in reduced[at]:
                copy.wait_recv()
            blocks = []
            for side in range(lat_count):
                block = arriving[0, side].astype(jnp.float32)
                for lev in range(1, lev_count):
                    block = block + arriving[lev, side].astype(jnp.float32)
                blocks.append(block.astype(jnp.bfloat16).astype(jnp.float32))
            return blocks
        for _ in arrivals("lat", crossed[at]):
            pass
        return [landed[side].astype(jnp.float32) for side in range(lat_count)]

    def start_return(at):
        rows, back, gathered, lat_sems = (buffers[at][n] for n in (4, 5, 6, 9))
        if at == last and direct:
            shared[at] = send_all(
                lambda lev, lat: rows.at[lat], gathered.at[lev_index, lat_index], direct_sems.at[1]
            )
            gathered[lev_index, lat_index] = rows[lat_index]
            finished.append(shared[at])
        else:
            returned[at] = send("lat", lambda peer: rows.at[peer], back.at[lat_index], lat_sems.at[1])
            back[lat_index] = rows[lat_index]
            finished.append(returned[at])

    def pass_on(at):
        if at in shared:
            return
        back, gathered, lev_sems = (buffers[at][n] for n in (5, 6, 8))
        for _ in arrivals("lat", returned[at]):
            pass
        shared[at] = send("lev", lambda peer: back, gathered.at[lev_index], lev_sems.at[1])
        gathered[lev_index] = back[...]
        finished.append(shared[at])

    project(0)
    expect(greetings)
    start_reduce(0)
    if last > 0:
        project(1)
        start_reduce(1)
    for at in range(2, len(chunks)):
        project(at)
    fill_constants(plan, deal, mixing_ref, keep, gather, placed_sign, mixer, sum_sign, spread, fold_keep)
    fill_tables(plan, device, lengths, deal, table, row_length)
    if not direct:
        start_cross(0)
    if last > 0:
        start_cross(1)
    if last > 1:
        start_reduce(2)
    fill_products(plan, device, row_length, deal, products, weights)

    for at, (first, count) in enumerate(chunks):
        rows = buffers[at][4]
        each = count // pack
        blocks = land(at)
        values = jnp.concatenate(
            [
                jnp.concatenate(
                    [block[:, part * part_span : (part + 1) * part_span] for block in blocks], axis=1
                )
                for part in range(pack)
            ],
            axis=0,
        )
        values = values * weights[0, first : first + count]
        values_ref[first : first + count] = values
        place_coefficients(plan, first, values, keep, gather, placed_sign, mixer, left)
        groups = list(range(first // plan.share, (first + count) // plan.share))
        walk_circles(plan, groups, device, lengths, table, left, total)
        if 0 < at < last:
            pass_on(at - 1)
        size = 2 * plan.block
        result = fold_circles(
            plan,
            total[first // plan.share * size : (first + count) // plan.share * size, :],
            sum_sign,
            spread,
            fold_keep,
        )
        values = values_ref[first : first + count]
        for other in range(plan.waves):
            result = result + products[other, first : first + count] * rolled(plan, values, other)
        result = result * weights[1, first : first + count]
        for side in range(lat_count):
            rows[side] = jnp.concatenate(
                [
                    result[part * each : (part + 1) * each, side * part_span : (side + 1) * part_span]
                    for part in range(pack)
                ],
                axis=1,
            ).astype(jnp.bfloat16)
        start_return(at)
        if at + 2 <= last:
            start_cross(at + 2)
            if at + 3 <= last:
                start_reduce(at + 3)
    if last > 0:
        pass_on(last - 1)

    sums = [None] * slots
    for at, (first, count) in enumerate(chunks):
        gathered, turned = buffers[at][6], buffers[at][7]
        each = count // pack
        pass_on(at)
        for copy in shared[at]:
            copy.wait_recv()
        for source in range(devices):
            block = gathered[source // lat_count, source % lat_count].astype(jnp.float32)
            for face in range(faces):
                turned[face, pl.ds(source, each, stride=devices), :] = block[:, face * BLK : (face + 1) * BLK]
        sides = [turned[face].astype(jnp.bfloat16) for face in range(faces)]
        for slot in range(slots):
            for part in range(pack):
                lane = part * part_span + slot * part_width
                start = (first + part * each) * devices
                value = jnp.dot(
                    held[slot, :, start : start + each * devices],
                    sides[lane // BLK],
                    preferred_element_type=jnp.float32,
                )[:, lane % BLK : lane % BLK + part_width]
                sums[slot] = value if sums[slot] is None else sums[slot] + value
    odd, masks = column_masks(plan, deal, slots, local_cols)
    for slot in range(slots):
        flat = sums[slot].T
        out_ref[slot] = (flat[: 2 * fields] + odd * flat[2 * fields :]) * masks[slot]
    for copies in finished:
        for copy in copies:
            copy.wait_send()


def local(spec_in, legendre, pattern, deal_list, circle_lengths, mixing):
    lat_count, lev_count = lax.axis_size("lat"), lax.axis_size("lev")
    slots, local_cols, half_lat = legendre.shape
    fields, waves = spec_in.shape[2], deal_list.shape[0]
    plan = Plan(waves, fields, lat_count, lev_count, half_lat)
    span = 4 * slots * fields
    pack = max(1, BLK // span)
    chunks = plan.chunks(pack)
    vmem = pl.BlockSpec(memory_space=pltpu.VMEM)
    smem = pl.BlockSpec(memory_space=pltpu.SMEM)
    size, wide = 2 * plan.block, 4 * plan.images
    scratch = [
        pltpu.VMEM(legendre.shape, jnp.bfloat16),
        pltpu.SemaphoreType.DMA((len(chunks),)),
        pltpu.VMEM((plan.groups, wide, plan.depth), jnp.bfloat16),
        pltpu.VMEM((plan.groups, 4, plan.block, BLK), jnp.float32),
        pltpu.VMEM((plan.groups * size, wide), jnp.float32),
        pltpu.VMEM((plan.rows, BLK), jnp.float32),
        pltpu.VMEM((waves, plan.rows, plan.lanes), jnp.float32),
        pltpu.VMEM((2, plan.rows, plan.lanes), jnp.float32),
        pltpu.VMEM((plan.rows, plan.lanes), jnp.float32),
        pltpu.VMEM((plan.hf, plan.lanes), jnp.float32),
        pltpu.VMEM((2 * plan.lanes, plan.depth), jnp.bfloat16),
        pltpu.VMEM((4, plan.images, plan.depth), jnp.float32),
        pltpu.VMEM((BLK, BLK), jnp.bfloat16),
        pltpu.VMEM((size, wide), jnp.float32),
        pltpu.VMEM((2 * wide, plan.lanes), jnp.bfloat16),
        pltpu.VMEM((size, plan.lanes), jnp.float32),
        pltpu.SemaphoreType.DMA((2, 2, min(plan.devices, DIRECT))),
    ]
    for _, count in chunks:
        scratch += chunk_scratch(count, pack, span * pack, lat_count, lev_count)
    product = pl.pallas_call(
        functools.partial(round_trip_kernel, plan, pack, chunks),
        out_shape=jax.ShapeDtypeStruct((slots, 2 * fields, local_cols), jnp.float32),
        in_specs=[smem, smem, vmem, pl.BlockSpec(memory_space=pl.ANY), vmem],
        out_specs=vmem,
        scratch_shapes=scratch,
        compiler_params=pltpu.CompilerParams(collective_id=0, has_side_effects=True),
    )(circle_lengths, deal_list, spec_in, legendre, mixing)
    return product.reshape(slots, 2, fields, local_cols)


def solution(mesh):
    return jax.shard_map(
        local,
        mesh=mesh,
        in_specs=(
            P("lat", None, None, "lev"),
            P("lat", "lev", None),
            P("lat", None, None),
            P(),
            P(),
            P(),
        ),
        out_specs=P("lat", None, None, "lev"),
        check_vma=False,
    )
```

```python
import functools
import math

import jax
import jax.numpy as jnp
from jax import lax
from jax.experimental import pallas as pl
from jax.experimental.pallas import tpu as pltpu
from jax.sharding import PartitionSpec as P

BLK = 128
SPAN = 2 * BLK
ACROSS = (((1,), (1,)), ((), ()))
STREAMS = 4
SPLIT = ((8, 10), (0, 6), (6, 8))
DIRECT = 64


def iota(shape, axis):
    return lax.broadcasted_iota(jnp.int32, shape, axis)


def unit(condition):
    return jnp.where(condition, 1.0, 0.0).astype(jnp.float32)


class Plan:
    def __init__(self, waves, fields, lat_count, lev_count, half_lat):
        self.waves, self.fields = waves, fields
        self.half_lat = half_lat
        self.devices = lat_count * lev_count
        self.rows = half_lat // self.devices
        self.hf = 2 * fields
        self.lanes = waves * 4 * fields
        self.share = max(
            n for n in range(1, self.rows + 1) if self.rows % n == 0 and (n == 1 or 4 * n * waves <= BLK)
        )
        self.groups = self.rows // self.share
        self.block = self.share * waves
        self.depth = 4 * self.block
        self.images = self.share * self.hf
        self.scale = (2.0 * waves) ** (-0.5)

    def tiles(self, group):
        needed = (group + 1) * self.share * self.devices + 5
        tiles = [(at, SPAN) for at in range(0, needed, SPAN)]
        if needed - tiles[-1][0] <= BLK:
            tiles[-1] = tiles[-1][0], BLK
        return tiles

    def inside(self, group, at, span):
        first = group * self.share * self.devices
        return at > 0 and at + span - 1 < 3 + first - first // 2

    def chunks(self, pack):
        least = pack
        while least * self.devices % (pack * BLK) or least % self.share:
            least += pack
        units = self.rows // least
        marks = [(units * start // 10 * least, units * stop // 10 * least) for start, stop in SPLIT]
        return [(start, stop - start) for start, stop in marks if stop > start]


def waves_at(deal, index, waves):
    out = jnp.zeros_like(index)
    for wave in range(waves):
        out = jnp.where(index == wave, deal[wave], out)
    return out


def circle_point(turns):
    quadrant = jnp.floor(4.0 * turns + 0.5)
    angle = (turns - 0.25 * quadrant) * (2.0 * math.pi)
    square = angle * angle
    sine = angle * (
        1.0 + square * (-1.0 / 6 + square * (1.0 / 120 + square * (-1.0 / 5040 + square * (1.0 / 362880))))
    )
    cosine = 1.0 + square * (
        -0.5 + square * (1.0 / 24 + square * (-1.0 / 720 + square * (1.0 / 40320 - square * (1.0 / 3628800))))
    )
    turned = (quadrant == 1.0) | (quadrant == 3.0)
    first, second = jnp.where(turned, sine, cosine), jnp.where(turned, cosine, sine)
    first = jnp.where((quadrant == 1.0) | (quadrant == 2.0), -first, first)
    second = jnp.where((quadrant == 2.0) | (quadrant == 3.0), -second, second)
    return first, second


def fill_tables(plan, device, lengths, deal, table, row_length):
    wave = waves_at(deal, iota((plan.block, BLK), 0) % plan.waves, plan.waves).astype(jnp.float32)
    product = wave * iota((plan.block, BLK), 1).astype(jnp.float32)
    member = iota((plan.block, BLK), 0) // plan.waves
    unroll = max(n for n in range(1, 6) if plan.groups % n == 0)

    def fill(step, carry):
        for near in range(unroll):
            group = step * unroll + near
            length = jnp.zeros((plan.block, BLK), jnp.float32)
            for each in range(plan.share):
                own = lengths[(group * plan.share + each) * plan.devices + device].astype(jnp.float32)
                length = jnp.where(member == each, own, length)
                row_length[pl.ds(group * plan.share + each, 1), :] = jnp.full((1, BLK), own, jnp.float32)
            inverse = 1.0 / length
            turned = product - jnp.floor(product * inverse) * length
            cosine, sine = circle_point(turned * inverse)
            last_cos, last_sin = cosine[:, BLK - 1 : BLK], sine[:, BLK - 1 : BLK]
            next_cos, next_sin = cosine[:, 1:2], sine[:, 1:2]
            table[group, 0] = cosine
            table[group, 1] = -sine
            table[group, 2] = jnp.broadcast_to(last_cos * next_cos - last_sin * next_sin, product.shape)
            table[group, 3] = jnp.broadcast_to(-last_sin * next_cos - last_cos * next_sin, product.shape)
            table[group, 4] = 0.25 * length + 0.5
        return carry

    lax.fori_loop(0, plan.groups // unroll, fill, 0)


def lane_waves(plan, deal):
    return waves_at(deal, iota((1, plan.lanes), 1) // (4 * plan.fields), plan.waves)


def live_rows(plan, device, deal):
    half_lat = plan.half_lat
    cut = lane_waves(plan, deal) * (half_lat // BLK) // (2 * half_lat)
    row = iota((plan.rows, 1), 0) * plan.devices + device
    return unit(row // BLK >= cut)


def image_sign(image, sine, odd):
    sign = jnp.ones(jnp.broadcast_shapes(sine.shape, odd.shape), jnp.float32)
    if image % 2:
        sign = sign * (1.0 - 2.0 * unit(sine))
    if image // 2:
        sign = sign * (1.0 - 2.0 * unit(odd))
    return sign


def fill_constants(plan, deal, mixing_ref, keep, gather, placed_sign, mixer, sum_sign, spread, fold_keep):
    waves, fields, hf, lanes = plan.waves, plan.fields, plan.hf, plan.lanes
    lane = iota((hf, lanes), 1)
    keep[...] = unit(lane // (2 * fields) % 2 * fields + lane % fields == iota((hf, lanes), 0))
    down, right = iota((2 * lanes, plan.depth), 0), iota((2 * lanes, plan.depth), 1)
    down_kind = down // lanes * 2 + down % lanes // fields % 2
    down_wave = down % lanes // (4 * fields)
    gather[...] = unit(
        (down_kind == right // plan.block) & (down_wave == right % waves)
    ).astype(jnp.bfloat16)
    right = iota((1, plan.depth), 1)
    mine = unit(iota((plan.images, 1), 0) // hf == right % plan.block // waves)
    odd = waves_at(deal, right % waves, waves) % 2 == 1
    sine = right // plan.block % 2 == 1
    for image in range(4):
        placed_sign[image] = mine * image_sign(image, sine, odd)
    pick = unit(iota((BLK, fields), 0) % fields == iota((BLK, fields), 1)).astype(jnp.bfloat16)
    half = lax.dot_general(
        pick, mixing_ref[...], ACROSS, preferred_element_type=jnp.float32
    ).astype(jnp.bfloat16)
    whole = lax.dot_general(half, pick, ACROSS, preferred_element_type=jnp.float32)
    same = iota((BLK, BLK), 0) // fields == iota((BLK, BLK), 1) // fields
    mixer[...] = jnp.where(same, whole, 0.0).astype(jnp.bfloat16)
    size, wide = sum_sign.shape
    down, right = iota((size, wide), 0), iota((size, wide), 1)
    odd = waves_at(deal, down % waves, waves) % 2 == 1
    sine = down // plan.block == 1
    sign = jnp.zeros((size, wide), jnp.float32)
    for image in range(4):
        sign = jnp.where(right // plan.images == image, image_sign(image, sine, odd), sign)
    sum_sign[...] = sign * unit(down % plan.block // waves == right % plan.images // hf)
    down, right = iota((2 * wide, lanes), 0), iota((2 * wide, lanes), 1)
    spread[...] = unit(
        down % hf == right // (2 * fields) % 2 * fields + right % fields
    ).astype(jnp.bfloat16)
    down, right = iota((size, lanes), 0), iota((size, lanes), 1)
    fold_keep[...] = unit(
        (down // plan.block == right // fields % 2) & (down % waves == right // (4 * fields))
    )


def fill_products(plan, device, row_length, deal, products, weights):
    length = jnp.concatenate([row_length[...]] * (plan.lanes // BLK), axis=1)
    wave = lane_waves(plan, deal).astype(jnp.float32)
    part = 1.0 - 2.0 * unit(iota((1, plan.lanes), 1) // plan.fields % 2 == 1)
    inverse, half = 1.0 / length, (0.5 * plan.scale) * length

    def whole(turns):
        return unit(turns == length * jnp.floor(turns * inverse + 0.5))

    for other in range(plan.waves):
        partner = rolled(plan, wave, other)
        products[other] = half * (whole(wave - partner) + part * whole(wave + partner))
    row = (iota((plan.rows, 1), 0) * plan.devices + device).astype(jnp.float32)
    weight = jnp.sin(math.pi * (row + 0.5) / (2 * plan.half_lat)) / jnp.sqrt(row_length[...])
    weights[0] = live_rows(plan, device, deal)
    weights[1] = weights[0] * jnp.concatenate([weight] * (plan.lanes // BLK), axis=1)


def rolled(plan, source, other):
    at = other * 4 * plan.fields
    return jnp.concatenate([source[:, at:], source[:, :at]], axis=1) if at else source


def place_coefficients(plan, first, values, keep, gather, placed_sign, mixer, left):
    rows = values.shape[0]
    narrow = values.astype(jnp.bfloat16)
    mixed = plan.scale * jnp.concatenate(
        [
            jnp.dot(narrow[:, at : at + BLK], mixer[...], preferred_element_type=jnp.float32)
            for at in range(0, plan.lanes, BLK)
        ],
        axis=1,
    )
    high = mixed.astype(jnp.bfloat16).astype(jnp.float32)
    spread = jnp.concatenate(
        [
            (source[:, None, :] * keep[...][None]).reshape(rows * plan.hf, plan.lanes).astype(jnp.bfloat16)
            for source in (high, mixed - high)
        ],
        axis=1,
    )
    placed = jnp.dot(spread, gather[...], preferred_element_type=jnp.float32)
    for group in range(rows // plan.share):
        own = placed[group * plan.images : (group + 1) * plan.images]
        for image in range(4):
            left[
                first // plan.share + group, image * plan.images : (image + 1) * plan.images, :
            ] = (own * placed_sign[image]).astype(jnp.bfloat16)


def walk_circles(plan, groups, table, left, total):
    position = iota((1, SPAN), 1).astype(jnp.float32)

    def phases(group, at, span, cos_now, sin_now):
        step_cos, step_sin = table[group, 2], table[group, 3]
        cosines, sines = [], []
        for _ in range(span // BLK):
            cosines.append(cos_now)
            sines.append(sin_now)
            cos_now, sin_now = (
                cos_now * step_cos - sin_now * step_sin,
                sin_now * step_cos + cos_now * step_sin,
            )
        cosine, sine = jnp.concatenate(cosines, axis=1), jnp.concatenate(sines, axis=1)
        near, far = cosine.astype(jnp.bfloat16), sine.astype(jnp.bfloat16)
        weights = jnp.concatenate([near, far, near, far], axis=0)
        if plan.inside(group, at, span):
            return cos_now, sin_now, weights, weights[: 2 * plan.block]
        limit = jnp.concatenate([table[group, 4]] * (span // BLK), axis=1)
        share = jnp.clip(limit - (position[:, :span] + float(at)), 0.0, 1.0)
        if at == 0:
            share = share * jnp.where(position[:, :span] == 0.0, 0.5, 1.0)
        shared = jnp.concatenate([cosine * share, sine * share], axis=0).astype(jnp.bfloat16)
        return cos_now, sin_now, weights, shared

    streams = [[] for _ in range(STREAMS)]
    for group in sorted(groups, key=lambda group: -len(plan.tiles(group))):
        min(streams, key=len).extend((group, at, span) for at, span in plan.tiles(group))
    state, sums, waiting = {}, {}, []

    def finish():
        for group, shared, grid in waiting:
            extra = lax.dot_general(
                shared,
                jnp.tanh(grid).astype(jnp.bfloat16),
                ACROSS,
                preferred_element_type=jnp.float32,
            )
            sums[group] = sums[group] + extra if group in sums else extra
        waiting.clear()

    for step in range(max(len(stream) for stream in streams)):
        started = []
        for stream in streams:
            if step < len(stream):
                group, at, span = stream[step]
                if group not in state:
                    state[group] = table[group, 0], table[group, 1]
                cos_now, sin_now, weights, shared = phases(group, at, span, *state[group])
                state[group] = cos_now, sin_now
                grid = jnp.dot(left[group], weights, preferred_element_type=jnp.float32)
                started.append((group, shared, grid))
        finish()
        waiting.extend(started)
    finish()
    size = 2 * plan.block
    for group in groups:
        total[group * size : (group + 1) * size, :] = sums[group]


def fold_circles(plan, sums, sum_sign, spread, fold_keep):
    size, wide = sum_sign.shape
    count = sums.shape[0] // size
    signed = (sums.reshape(count, size, wide) * sum_sign[...][None]).reshape(count * size, wide)
    high = signed.astype(jnp.bfloat16)
    low = (signed - high.astype(jnp.float32)).astype(jnp.bfloat16)
    folded = jnp.dot(
        jnp.concatenate([high, low], axis=1), spread[...], preferred_element_type=jnp.float32
    )
    kept = (folded.reshape(count, size, plan.lanes) * fold_keep[...][None]).reshape(
        count, 2, plan.share, plan.waves, plan.lanes
    )
    return jnp.sum(jnp.sum(kept, axis=1), axis=2).reshape(count * plan.share, plan.lanes)


def column_masks(plan, deal, slots, local_cols):
    column = iota((1, local_cols), 1) + lax.axis_index("lev") * local_cols
    odd = (1 - 2 * (column % 2)).astype(jnp.float32)
    masks = []
    for slot in range(slots):
        wave = deal[lax.axis_index("lat") * slots + slot]
        masks.append(unit(column // BLK * BLK <= plan.half_lat - 1 - wave))
    return odd, masks


def peers_of(axis):
    count = lax.axis_size(axis)
    return [lax.rem(lax.axis_index(axis) + off, count) for off in range(1, count)]


def expect(total):
    pl.semaphore_wait(pltpu.get_barrier_semaphore(), total)


def others(count):
    lat_count = lax.axis_size("lat")
    me = lax.axis_index("lev") * lat_count + lax.axis_index("lat")
    for off in range(1, count):
        peer = lax.rem(me + off, count)
        yield {"lat": lax.rem(peer, lat_count), "lev": lax.div(peer, lat_count)}


def hail(direct):
    barrier = pltpu.get_barrier_semaphore()
    if direct:
        peers = list(others(lax.axis_size("lat") * lax.axis_size("lev")))
    else:
        peers = [{axis: peer} for axis in ("lat", "lev") for peer in peers_of(axis)]
    for peer in peers:
        pl.semaphore_signal(barrier, inc=1, device_id=peer, device_id_type=pl.DeviceIdType.MESH)
    return len(peers)


def send_all(sources, target, sems):
    copies = []
    for step, peer in enumerate(others(lax.axis_size("lat") * lax.axis_size("lev"))):
        copy = pltpu.make_async_remote_copy(
            src_ref=sources(peer["lev"], peer["lat"]),
            dst_ref=target,
            send_sem=sems.at[0, step],
            recv_sem=sems.at[1, step],
            device_id=peer,
            device_id_type=pl.DeviceIdType.MESH,
        )
        copy.start()
        copies.append(copy)
    return copies


def send(axis, sources, target, sems):
    copies = []
    for step, peer in enumerate(peers_of(axis)):
        copy = pltpu.make_async_remote_copy(
            src_ref=sources(peer),
            dst_ref=target,
            send_sem=sems.at[0, step],
            recv_sem=sems.at[1, step],
            device_id={axis: peer},
            device_id_type=pl.DeviceIdType.MESH,
        )
        copy.start()
        copies.append(copy)
    return copies


def arrivals(axis, copies):
    count, index = lax.axis_size(axis), lax.axis_index(axis)
    for off, copy in enumerate(copies, 1):
        copy.wait_recv()
        yield lax.rem(index + count - off, count)


def chunk_scratch(count, pack, width, lat_count, lev_count):
    block = (lat_count, count // pack, width)
    devices = lat_count * lev_count
    return [
        pltpu.VMEM((lev_count,) + block, jnp.bfloat16),
        pltpu.VMEM((lev_count,) + block, jnp.bfloat16),
        pltpu.VMEM(block, jnp.bfloat16),
        pltpu.VMEM(block, jnp.bfloat16),
        pltpu.VMEM(block, jnp.bfloat16),
        pltpu.VMEM(block, jnp.bfloat16),
        pltpu.VMEM((lev_count,) + block, jnp.bfloat16),
        pltpu.VMEM((width // BLK, count // pack * devices, BLK), jnp.float32),
        pltpu.SemaphoreType.DMA((2, 2, lev_count)),
        pltpu.SemaphoreType.DMA((2, 2, lat_count)),
    ]


CHUNK_REFS = 10


def round_trip_kernel(
    plan, pack, chunks, lengths_in, deal_in, spec_in, legendre_ref, mixing_in, out_ref, *scratch
):
    held, load_sems, left, table, total, row_length, products, weights, values_ref = scratch[:9]
    keep, gather, placed_sign, mixer, sum_sign, spread, fold_keep, direct_sems = scratch[9:17]
    lengths, deal, spec_ref, mixing_ref, input_sems = scratch[17:22]
    buffers = [
        scratch[22 + at * CHUNK_REFS : 22 + (at + 1) * CHUNK_REFS] for at in range(len(chunks))
    ]
    slots, local_cols, half_lat = held.shape
    fields, devices = plan.fields, plan.devices
    lat_count, lev_count = lax.axis_size("lat"), lax.axis_size("lev")
    lev_index, lat_index = lax.axis_index("lev"), lax.axis_index("lat")
    device = lev_index * lat_count + lat_index
    part_width = 4 * fields
    part_span = slots * part_width
    width = part_span * pack
    faces = width // BLK
    last = len(chunks) - 1
    direct = devices <= DIRECT
    greetings = hail(direct)
    inputs = [
        pltpu.make_async_copy(source, target, input_sems.at[at])
        for at, (source, target) in enumerate(
            ((deal_in, deal), (spec_in, spec_ref), (lengths_in, lengths), (mixing_in, mixing_ref))
        )
    ]
    for load in inputs:
        load.start()
    loads = []
    for at, (first, count) in enumerate(chunks):
        columns = pl.ds(first * devices, count * devices)
        load = pltpu.make_async_copy(
            legendre_ref.at[:, :, columns], held.at[:, :, columns], load_sems.at[at]
        )
        load.start()
        loads.append(load)
    inputs[0].wait()
    inputs[1].wait()
    odd, masks = column_masks(plan, deal, slots, local_cols)
    lefts = []
    for slot in range(slots):
        kept = jnp.concatenate([spec_ref[slot, 0], spec_ref[slot, 1]], axis=0).astype(jnp.float32)
        kept = kept * masks[slot]
        lefts.append(jnp.concatenate([kept, kept * odd], axis=0).astype(jnp.bfloat16))

    finished = []
    reduced, crossed, returned, shared = {}, {}, {}, {}

    def project(at):
        first, count = chunks[at]
        leaving, turned = buffers[at][0], buffers[at][7]
        each = count // pack
        loads[at].wait()
        sums = [
            jnp.dot(
                lefts[slot],
                held[slot, :, first * devices : (first + count) * devices],
                preferred_element_type=jnp.float32,
            )
            for slot in range(slots)
        ]
        for block in range(each * devices // BLK):
            piece = jnp.concatenate(
                [
                    value[:, part * each * devices + block * BLK : part * each * devices + (block + 1) * BLK]
                    for part in range(pack)
                    for value in sums
                ],
                axis=0,
            )
            for face in range(faces):
                turned[face, block * BLK : (block + 1) * BLK, :] = piece[face * BLK : (face + 1) * BLK].T
        for target in range(devices):
            for face in range(faces):
                leaving[target // lat_count, target % lat_count, :, face * BLK : (face + 1) * BLK] = (
                    turned[face, pl.ds(target, each, stride=devices), :].astype(jnp.bfloat16)
                )

    def start_reduce(at):
        leaving, arriving, lev_sems = (buffers[at][n] for n in (0, 1, 8))
        if at == 0 and direct:
            copies = send_all(
                lambda lev, lat: leaving.at[lev, lat], arriving.at[lev_index, lat_index], direct_sems.at[0]
            )
            arriving[lev_index, lat_index] = leaving[lev_index, lat_index]
        else:
            copies = send("lev", lambda peer: leaving.at[peer], arriving.at[lev_index], lev_sems.at[0])
        reduced[at] = copies
        finished.append(copies)

    def start_cross(at):
        count = chunks[at][1]
        arriving, summed, landed, turned, lat_sems = (buffers[at][n] for n in (1, 2, 3, 7, 9))
        each = count // pack
        total_of = jnp.stack(
            [
                jnp.concatenate(
                    [
                        turned[face, pl.ds(lev_index * lat_count + side, each, stride=devices), :]
                        for face in range(faces)
                    ],
                    axis=1,
                )
                for side in range(lat_count)
            ]
        )
        for peer in arrivals("lev", reduced[at]):
            total_of = total_of + arriving[peer].astype(jnp.float32)
        summed[...] = total_of.astype(jnp.bfloat16)
        crossed[at] = send("lat", lambda peer: summed.at[peer], landed.at[lat_index], lat_sems.at[0])
        landed[lat_index] = summed[lat_index]
        finished.append(crossed[at])

    def land(at):
        arriving, landed = buffers[at][1], buffers[at][3]
        if at == 0 and direct:
            for copy in reduced[at]:
                copy.wait_recv()
            blocks = []
            for side in range(lat_count):
                block = arriving[0, side].astype(jnp.float32)
                for lev in range(1, lev_count):
                    block = block + arriving[lev, side].astype(jnp.float32)
                blocks.append(block.astype(jnp.bfloat16).astype(jnp.float32))
            return blocks
        for _ in arrivals("lat", crossed[at]):
            pass
        return [landed[side].astype(jnp.float32) for side in range(lat_count)]

    def start_return(at):
        rows, back, gathered, lat_sems = (buffers[at][n] for n in (4, 5, 6, 9))
        if at == last and direct:
            shared[at] = send_all(
                lambda lev, lat: rows.at[lat], gathered.at[lev_index, lat_index], direct_sems.at[1]
            )
            gathered[lev_index, lat_index] = rows[lat_index]
            finished.append(shared[at])
        else:
            returned[at] = send("lat", lambda peer: rows.at[peer], back.at[lat_index], lat_sems.at[1])
            back[lat_index] = rows[lat_index]
            finished.append(returned[at])

    def pass_on(at):
        if at in shared:
            return
        back, gathered, lev_sems = (buffers[at][n] for n in (5, 6, 8))
        for _ in arrivals("lat", returned[at]):
            pass
        shared[at] = send("lev", lambda peer: back, gathered.at[lev_index], lev_sems.at[1])
        gathered[lev_index] = back[...]
        finished.append(shared[at])

    project(0)
    inputs[2].wait()
    inputs[3].wait()
    fill_constants(plan, deal, mixing_ref, keep, gather, placed_sign, mixer, sum_sign, spread, fold_keep)
    fill_tables(plan, device, lengths, deal, table, row_length)
    expect(greetings)
    start_reduce(0)
    if last > 0:
        project(1)
        start_reduce(1)
    for at in range(2, len(chunks)):
        project(at)
    if not direct:
        start_cross(0)
    if last > 0:
        start_cross(1)
    if last > 1:
        start_reduce(2)
    fill_products(plan, device, row_length, deal, products, weights)

    for at, (first, count) in enumerate(chunks):
        rows = buffers[at][4]
        each = count // pack
        blocks = land(at)
        values = jnp.concatenate(
            [
                jnp.concatenate(
                    [block[:, part * part_span : (part + 1) * part_span] for block in blocks], axis=1
                )
                for part in range(pack)
            ],
            axis=0,
        )
        values = values * weights[0, first : first + count]
        values_ref[first : first + count] = values
        place_coefficients(plan, first, values, keep, gather, placed_sign, mixer, left)
        groups = list(range(first // plan.share, (first + count) // plan.share))
        walk_circles(plan, groups, table, left, total)
        if 0 < at < last:
            pass_on(at - 1)
        size = 2 * plan.block
        result = fold_circles(
            plan,
            total[first // plan.share * size : (first + count) // plan.share * size, :],
            sum_sign,
            spread,
            fold_keep,
        )
        values = values_ref[first : first + count]
        for other in range(plan.waves):
            result = result + products[other, first : first + count] * rolled(plan, values, other)
        result = result * weights[1, first : first + count]
        for side in range(lat_count):
            rows[side] = jnp.concatenate(
                [
                    result[part * each : (part + 1) * each, side * part_span : (side + 1) * part_span]
                    for part in range(pack)
                ],
                axis=1,
            ).astype(jnp.bfloat16)
        start_return(at)
        if at + 2 <= last:
            start_cross(at + 2)
            if at + 3 <= last:
                start_reduce(at + 3)
    if last > 0:
        pass_on(last - 1)

    sums = [None] * slots
    for at, (first, count) in enumerate(chunks):
        gathered, turned = buffers[at][6], buffers[at][7]
        each = count // pack
        pass_on(at)
        for copy in shared[at]:
            copy.wait_recv()
        for source in range(devices):
            block = gathered[source // lat_count, source % lat_count].astype(jnp.float32)
            for face in range(faces):
                turned[face, pl.ds(source, each, stride=devices), :] = block[:, face * BLK : (face + 1) * BLK]
        sides = [turned[face].astype(jnp.bfloat16) for face in range(faces)]
        for slot in range(slots):
            for part in range(pack):
                lane = part * part_span + slot * part_width
                start = (first + part * each) * devices
                value = jnp.dot(
                    held[slot, :, start : start + each * devices],
                    sides[lane // BLK],
                    preferred_element_type=jnp.float32,
                )[:, lane % BLK : lane % BLK + part_width]
                sums[slot] = value if sums[slot] is None else sums[slot] + value
    odd, masks = column_masks(plan, deal, slots, local_cols)
    for slot in range(slots):
        flat = sums[slot].T
        out_ref[slot] = (flat[: 2 * fields] + odd * flat[2 * fields :]) * masks[slot]
    for copies in finished:
        for copy in copies:
            copy.wait_send()


def local(spec_in, legendre, pattern, deal_list, circle_lengths, mixing):
    lat_count, lev_count = lax.axis_size("lat"), lax.axis_size("lev")
    slots, local_cols, half_lat = legendre.shape
    fields, waves = spec_in.shape[2], deal_list.shape[0]
    plan = Plan(waves, fields, lat_count, lev_count, half_lat)
    span = 4 * slots * fields
    pack = max(1, BLK // span)
    chunks = plan.chunks(pack)
    vmem = pl.BlockSpec(memory_space=pltpu.VMEM)
    size, wide = 2 * plan.block, 4 * plan.images
    scratch = [
        pltpu.VMEM(legendre.shape, jnp.bfloat16),
        pltpu.SemaphoreType.DMA((len(chunks),)),
        pltpu.VMEM((plan.groups, wide, plan.depth), jnp.bfloat16),
        pltpu.VMEM((plan.groups, 5, plan.block, BLK), jnp.float32),
        pltpu.VMEM((plan.groups * size, wide), jnp.float32),
        pltpu.VMEM((plan.rows, BLK), jnp.float32),
        pltpu.VMEM((waves, plan.rows, plan.lanes), jnp.float32),
        pltpu.VMEM((2, plan.rows, plan.lanes), jnp.float32),
        pltpu.VMEM((plan.rows, plan.lanes), jnp.float32),
        pltpu.VMEM((plan.hf, plan.lanes), jnp.float32),
        pltpu.VMEM((2 * plan.lanes, plan.depth), jnp.bfloat16),
        pltpu.VMEM((4, plan.images, plan.depth), jnp.float32),
        pltpu.VMEM((BLK, BLK), jnp.bfloat16),
        pltpu.VMEM((size, wide), jnp.float32),
        pltpu.VMEM((2 * wide, plan.lanes), jnp.bfloat16),
        pltpu.VMEM((size, plan.lanes), jnp.float32),
        pltpu.SemaphoreType.DMA((2, 2, min(plan.devices, DIRECT))),
        pltpu.SMEM(circle_lengths.shape, jnp.int32),
        pltpu.SMEM(deal_list.shape, jnp.int32),
        pltpu.VMEM(spec_in.shape, jnp.bfloat16),
        pltpu.VMEM(mixing.shape, jnp.bfloat16),
        pltpu.SemaphoreType.DMA((4,)),
    ]
    for _, count in chunks:
        scratch += chunk_scratch(count, pack, span * pack, lat_count, lev_count)
    product = pl.pallas_call(
        functools.partial(round_trip_kernel, plan, pack, chunks),
        out_shape=jax.ShapeDtypeStruct((slots, 2 * fields, local_cols), jnp.float32),
        in_specs=[pl.BlockSpec(memory_space=pl.ANY)] * 5,
        out_specs=vmem,
        scratch_shapes=scratch,
        compiler_params=pltpu.CompilerParams(collective_id=0, has_side_effects=True),
    )(circle_lengths, deal_list, spec_in, legendre, mixing)
    return product.reshape(slots, 2, fields, local_cols)


def solution(mesh):
    return jax.shard_map(
        local,
        mesh=mesh,
        in_specs=(
            P("lat", None, None, "lev"),
            P("lat", "lev", None),
            P("lat", None, None),
            P(),
            P(),
            P(),
        ),
        out_specs=P("lat", None, None, "lev"),
        check_vma=False,
    )
```

```python
import functools
import math

import jax
import jax.numpy as jnp
from jax import lax
from jax.experimental import pallas as pl
from jax.experimental.pallas import tpu as pltpu
from jax.sharding import PartitionSpec as P

BLK = 128
SPAN = 2 * BLK
ACROSS = (((1,), (1,)), ((), ()))
STREAMS = 2
SPLIT = ((8, 10), (0, 4), (4, 8))
DIRECT = 64


def iota(shape, axis):
    return lax.broadcasted_iota(jnp.int32, shape, axis)


def unit(condition):
    return jnp.where(condition, 1.0, 0.0).astype(jnp.float32)


class Plan:
    def __init__(self, waves, fields, lat_count, lev_count, half_lat):
        self.waves, self.fields = waves, fields
        self.half_lat = half_lat
        self.devices = lat_count * lev_count
        self.rows = half_lat // self.devices
        self.hf = 2 * fields
        self.lanes = waves * 4 * fields
        self.share = max(
            n for n in range(1, self.rows + 1) if self.rows % n == 0 and (n == 1 or 4 * n * waves <= BLK)
        )
        self.groups = self.rows // self.share
        self.block = self.share * waves
        self.depth = 4 * self.block
        self.images = self.share * self.hf
        self.own = 4 * self.hf
        self.face = max(BLK, self.own)
        self.scale = (2.0 * waves) ** (-0.5)

    def tiles(self, group):
        needed = (group + 1) * self.share * self.devices + 5
        tiles = [(at, SPAN) for at in range(0, needed, SPAN)]
        if needed - tiles[-1][0] <= BLK:
            tiles[-1] = tiles[-1][0], BLK
        return tiles

    def inside(self, group, at, span):
        first = group * self.share * self.devices
        return at > 0 and at + span - 1 < 3 + first - first // 2

    def chunks(self, pack):
        least = pack
        while least * self.devices % (pack * BLK) or least % self.share:
            least += pack
        units = self.rows // least
        marks = [(units * start // 10 * least, units * stop // 10 * least) for start, stop in SPLIT]
        return [(start, stop - start) for start, stop in marks if stop > start]


def waves_at(deal, index, waves):
    out = jnp.zeros_like(index)
    for wave in range(waves):
        out = jnp.where(index == wave, deal[wave], out)
    return out


def circle_point(turns):
    quadrant = jnp.floor(4.0 * turns + 0.5)
    angle = (turns - 0.25 * quadrant) * (2.0 * math.pi)
    square = angle * angle
    sine = angle * (
        1.0 + square * (-1.0 / 6 + square * (1.0 / 120 + square * (-1.0 / 5040 + square * (1.0 / 362880))))
    )
    cosine = 1.0 + square * (
        -0.5 + square * (1.0 / 24 + square * (-1.0 / 720 + square * (1.0 / 40320 - square * (1.0 / 3628800))))
    )
    turned = (quadrant == 1.0) | (quadrant == 3.0)
    first, second = jnp.where(turned, sine, cosine), jnp.where(turned, cosine, sine)
    first = jnp.where((quadrant == 1.0) | (quadrant == 2.0), -first, first)
    second = jnp.where((quadrant == 2.0) | (quadrant == 3.0), -second, second)
    return first, second


def fill_tables(plan, device, lengths, deal, table, row_length):
    wave = waves_at(deal, iota((plan.block, BLK), 0) % plan.waves, plan.waves).astype(jnp.float32)
    product = wave * iota((plan.block, BLK), 1).astype(jnp.float32)
    member = iota((plan.block, BLK), 0) // plan.waves
    unroll = max(n for n in range(1, 6) if plan.groups % n == 0)

    def fill(step, carry):
        for near in range(unroll):
            group = step * unroll + near
            length = jnp.zeros((plan.block, BLK), jnp.float32)
            for each in range(plan.share):
                own = lengths[(group * plan.share + each) * plan.devices + device].astype(jnp.float32)
                length = jnp.where(member == each, own, length)
                row_length[pl.ds(group * plan.share + each, 1), :] = jnp.full((1, BLK), own, jnp.float32)
            inverse = 1.0 / length
            turned = product - jnp.floor(product * inverse) * length
            cosine, sine = circle_point(turned * inverse)
            last_cos, last_sin = cosine[:, BLK - 1 : BLK], sine[:, BLK - 1 : BLK]
            next_cos, next_sin = cosine[:, 1:2], sine[:, 1:2]
            table[group, 0] = cosine
            table[group, 1] = -sine
            table[group, 2] = jnp.broadcast_to(last_cos * next_cos - last_sin * next_sin, product.shape)
            table[group, 3] = jnp.broadcast_to(-last_sin * next_cos - last_cos * next_sin, product.shape)
            table[group, 4] = 0.25 * length + 0.5
        return carry

    lax.fori_loop(0, plan.groups // unroll, fill, 0)


def lane_waves(plan, deal):
    return waves_at(deal, iota((1, plan.lanes), 1) // (4 * plan.fields), plan.waves)


def live_rows(plan, device, deal):
    half_lat = plan.half_lat
    cut = lane_waves(plan, deal) * (half_lat // BLK) // (2 * half_lat)
    row = iota((plan.rows, 1), 0) * plan.devices + device
    return unit(row // BLK >= cut)


def image_sign(image, sine, odd):
    sign = jnp.ones(jnp.broadcast_shapes(sine.shape, odd.shape), jnp.float32)
    if image % 2:
        sign = sign * (1.0 - 2.0 * unit(sine))
    if image // 2:
        sign = sign * (1.0 - 2.0 * unit(odd))
    return sign


def fill_constants(plan, deal, mixing_ref, keep, gather, placed_sign, mixer, sum_sign, spread, fold_keep):
    waves, fields, hf, lanes = plan.waves, plan.fields, plan.hf, plan.lanes
    lane = iota((hf, lanes), 1)
    keep[...] = unit(lane // (2 * fields) % 2 * fields + lane % fields == iota((hf, lanes), 0))
    down, right = iota((2 * lanes, plan.depth), 0), iota((2 * lanes, plan.depth), 1)
    down_kind = down // lanes * 2 + down % lanes // fields % 2
    down_wave = down % lanes // (4 * fields)
    gather[...] = unit(
        (down_kind == right // plan.block) & (down_wave == right % waves)
    ).astype(jnp.bfloat16)
    right = iota((1, plan.depth), 1)
    mine = unit(iota((plan.images, 1), 0) // hf == right % plan.block // waves)
    odd = waves_at(deal, right % waves, waves) % 2 == 1
    sine = right // plan.block % 2 == 1
    for image in range(4):
        placed_sign[image] = mine * image_sign(image, sine, odd)
    pick = unit(iota((BLK, fields), 0) % fields == iota((BLK, fields), 1)).astype(jnp.bfloat16)
    half = lax.dot_general(
        pick, mixing_ref[...], ACROSS, preferred_element_type=jnp.float32
    ).astype(jnp.bfloat16)
    whole = lax.dot_general(half, pick, ACROSS, preferred_element_type=jnp.float32)
    same = iota((BLK, BLK), 0) // fields == iota((BLK, BLK), 1) // fields
    mixer[...] = jnp.where(same, whole, 0.0).astype(jnp.bfloat16)
    size, wide = sum_sign.shape
    down, right = iota((size, wide), 0), iota((size, wide), 1)
    each = down // (2 * waves)
    lane = each * plan.own // plan.face * plan.face + right
    odd = waves_at(deal, down % waves, waves) % 2 == 1
    sine = down // waves % 2 == 1
    sign = jnp.zeros((size, wide), jnp.float32)
    for image in range(4):
        sign = jnp.where(lane % plan.own // hf == image, image_sign(image, sine, odd), sign)
    sum_sign[...] = sign * unit(each == lane // plan.own)
    down, right = iota((2 * wide, lanes), 0), iota((2 * wide, lanes), 1)
    spread[...] = unit(
        down % hf == right // (2 * fields) % 2 * fields + right % fields
    ).astype(jnp.bfloat16)
    down, right = iota((size, lanes), 0), iota((size, lanes), 1)
    fold_keep[...] = unit(
        (down // waves % 2 == right // fields % 2) & (down % waves == right // (4 * fields))
    )


def fill_products(plan, device, row_length, deal, products, weights):
    length = jnp.concatenate([row_length[...]] * (plan.lanes // BLK), axis=1)
    wave = lane_waves(plan, deal).astype(jnp.float32)
    part = 1.0 - 2.0 * unit(iota((1, plan.lanes), 1) // plan.fields % 2 == 1)
    inverse, half = 1.0 / length, (0.5 * plan.scale) * length

    def whole(turns):
        return unit(turns == length * jnp.floor(turns * inverse + 0.5))

    for other in range(plan.waves):
        partner = rolled(plan, wave, other)
        products[other] = half * (whole(wave - partner) + part * whole(wave + partner))
    row = (iota((plan.rows, 1), 0) * plan.devices + device).astype(jnp.float32)
    weight = jnp.sin(math.pi * (row + 0.5) / (2 * plan.half_lat)) / jnp.sqrt(row_length[...])
    weights[0] = live_rows(plan, device, deal)
    weights[1] = weights[0] * jnp.concatenate([weight] * (plan.lanes // BLK), axis=1)


def rolled(plan, source, other):
    at = other * 4 * plan.fields
    return jnp.concatenate([source[:, at:], source[:, :at]], axis=1) if at else source


def place_coefficients(plan, first, values, keep, gather, placed_sign, mixer, left):
    rows = values.shape[0]
    narrow = values.astype(jnp.bfloat16)
    mixed = plan.scale * jnp.concatenate(
        [
            jnp.dot(narrow[:, at : at + BLK], mixer[...], preferred_element_type=jnp.float32)
            for at in range(0, plan.lanes, BLK)
        ],
        axis=1,
    )
    high = mixed.astype(jnp.bfloat16).astype(jnp.float32)
    spread = jnp.concatenate(
        [
            (source[:, None, :] * keep[...][None]).reshape(rows * plan.hf, plan.lanes).astype(jnp.bfloat16)
            for source in (high, mixed - high)
        ],
        axis=1,
    )
    placed = jnp.dot(spread, gather[...], preferred_element_type=jnp.float32)
    for group in range(rows // plan.share):
        for each in range(plan.share):
            at = (group * plan.share + each) * plan.hf
            for image in range(4):
                to = each * plan.own + image * plan.hf
                left[first // plan.share + group, to : to + plan.hf, :] = (
                    placed[at : at + plan.hf] * placed_sign[image, each * plan.hf : (each + 1) * plan.hf, :]
                ).astype(jnp.bfloat16)


def walk_circles(plan, groups, table, left, total):
    position = iota((1, SPAN), 1).astype(jnp.float32)

    def phases(group, at, span, cos_now, sin_now):
        step_cos, step_sin = table[group, 2], table[group, 3]
        cosines, sines = [], []
        for _ in range(span // BLK):
            cosines.append(cos_now)
            sines.append(sin_now)
            cos_now, sin_now = (
                cos_now * step_cos - sin_now * step_sin,
                sin_now * step_cos + cos_now * step_sin,
            )
        cosine, sine = jnp.concatenate(cosines, axis=1), jnp.concatenate(sines, axis=1)
        near, far = cosine.astype(jnp.bfloat16), sine.astype(jnp.bfloat16)
        weights = jnp.concatenate([near, far, near, far], axis=0)
        if plan.inside(group, at, span):
            return cos_now, sin_now, weights, weights[: 2 * plan.block]
        limit = jnp.concatenate([table[group, 4]] * (span // BLK), axis=1)
        share = jnp.clip(limit - (position[:, :span] + float(at)), 0.0, 1.0)
        if at == 0:
            share = share * jnp.where(position[:, :span] == 0.0, 0.5, 1.0)
        shared = jnp.concatenate([cosine * share, sine * share], axis=0).astype(jnp.bfloat16)
        return cos_now, sin_now, weights, shared

    streams = [[] for _ in range(STREAMS)]
    for group in sorted(groups, key=lambda group: -len(plan.tiles(group))):
        min(streams, key=len).extend((group, at, span) for at, span in plan.tiles(group))
    state, sums, waiting = {}, {}, []

    def finish():
        for group, shared, grid in waiting:
            extra = lax.dot_general(
                shared,
                jnp.tanh(grid).astype(jnp.bfloat16),
                ACROSS,
                preferred_element_type=jnp.float32,
            )
            parts = []
            for each in range(plan.share):
                side = each * plan.own // plan.face * plan.face
                for row in (each * plan.waves, plan.block + each * plan.waves):
                    parts.append(extra[row : row + plan.waves, side : side + plan.face])
            if group in sums:
                parts = [old + new for old, new in zip(sums[group], parts)]
            sums[group] = parts
        waiting.clear()

    for step in range(max(len(stream) for stream in streams)):
        started = []
        for stream in streams:
            if step < len(stream):
                group, at, span = stream[step]
                if group not in state:
                    state[group] = table[group, 0], table[group, 1]
                cos_now, sin_now, weights, shared = phases(group, at, span, *state[group])
                state[group] = cos_now, sin_now
                grid = jnp.dot(left[group], weights, preferred_element_type=jnp.float32)
                started.append((group, shared, grid))
        finish()
        waiting.extend(started)
    finish()
    size = 2 * plan.block
    for group in groups:
        for at, part in enumerate(sums[group]):
            total[group * size + at * plan.waves : group * size + (at + 1) * plan.waves, :] = part


def fold_circles(plan, sums, sum_sign, spread, fold_keep):
    size, wide = sum_sign.shape
    count = sums.shape[0] // size
    signed = (sums.reshape(count, size, wide) * sum_sign[...][None]).reshape(count * size, wide)
    high = signed.astype(jnp.bfloat16)
    low = (signed - high.astype(jnp.float32)).astype(jnp.bfloat16)
    folded = jnp.dot(
        jnp.concatenate([high, low], axis=1), spread[...], preferred_element_type=jnp.float32
    )
    kept = (folded.reshape(count, size, plan.lanes) * fold_keep[...][None]).reshape(
        count * plan.share, 2, plan.waves, plan.lanes
    )
    return jnp.sum(jnp.sum(kept, axis=1), axis=1)


def column_masks(plan, deal, slots, local_cols):
    column = iota((1, local_cols), 1) + lax.axis_index("lev") * local_cols
    odd = (1 - 2 * (column % 2)).astype(jnp.float32)
    masks = []
    for slot in range(slots):
        wave = deal[lax.axis_index("lat") * slots + slot]
        masks.append(unit(column // BLK * BLK <= plan.half_lat - 1 - wave))
    return odd, masks


def peers_of(axis):
    count = lax.axis_size(axis)
    return [lax.rem(lax.axis_index(axis) + off, count) for off in range(1, count)]


def expect(total):
    pl.semaphore_wait(pltpu.get_barrier_semaphore(), total)


def others(count):
    lat_count = lax.axis_size("lat")
    me = lax.axis_index("lev") * lat_count + lax.axis_index("lat")
    for off in range(1, count):
        peer = lax.rem(me + off, count)
        yield {"lat": lax.rem(peer, lat_count), "lev": lax.div(peer, lat_count)}


def hail(direct):
    barrier = pltpu.get_barrier_semaphore()
    if direct:
        peers = list(others(lax.axis_size("lat") * lax.axis_size("lev")))
    else:
        peers = [{axis: peer} for axis in ("lat", "lev") for peer in peers_of(axis)]
    for peer in peers:
        pl.semaphore_signal(barrier, inc=1, device_id=peer, device_id_type=pl.DeviceIdType.MESH)
    return len(peers)


def send_all(sources, target, sems):
    copies = []
    for step, peer in enumerate(others(lax.axis_size("lat") * lax.axis_size("lev"))):
        copy = pltpu.make_async_remote_copy(
            src_ref=sources(peer["lev"], peer["lat"]),
            dst_ref=target,
            send_sem=sems.at[0, step],
            recv_sem=sems.at[1, step],
            device_id=peer,
            device_id_type=pl.DeviceIdType.MESH,
        )
        copy.start()
        copies.append(copy)
    return copies


def send(axis, sources, target, sems):
    copies = []
    for step, peer in enumerate(peers_of(axis)):
        copy = pltpu.make_async_remote_copy(
            src_ref=sources(peer),
            dst_ref=target,
            send_sem=sems.at[0, step],
            recv_sem=sems.at[1, step],
            device_id={axis: peer},
            device_id_type=pl.DeviceIdType.MESH,
        )
        copy.start()
        copies.append(copy)
    return copies


def arrivals(axis, copies):
    count, index = lax.axis_size(axis), lax.axis_index(axis)
    for off, copy in enumerate(copies, 1):
        copy.wait_recv()
        yield lax.rem(index + count - off, count)


def chunk_scratch(count, pack, width, lat_count, lev_count):
    block = (lat_count, count // pack, width)
    devices = lat_count * lev_count
    return [
        pltpu.VMEM((lev_count,) + block, jnp.bfloat16),
        pltpu.VMEM((lev_count,) + block, jnp.bfloat16),
        pltpu.VMEM(block, jnp.bfloat16),
        pltpu.VMEM(block, jnp.bfloat16),
        pltpu.VMEM(block, jnp.bfloat16),
        pltpu.VMEM(block, jnp.bfloat16),
        pltpu.VMEM((lev_count,) + block, jnp.bfloat16),
        pltpu.VMEM((width // BLK, count // pack * devices, BLK), jnp.float32),
        pltpu.SemaphoreType.DMA((2, 2, lev_count)),
        pltpu.SemaphoreType.DMA((2, 2, lat_count)),
    ]


CHUNK_REFS = 10


def round_trip_kernel(
    plan, pack, chunks, lengths_in, deal_in, spec_in, legendre_ref, mixing_in, out_ref, *scratch
):
    held, load_sems, left, table, total, row_length, products, weights, values_ref = scratch[:9]
    keep, gather, placed_sign, mixer, sum_sign, spread, fold_keep, direct_sems = scratch[9:17]
    lengths, deal, spec_ref, mixing_ref, input_sems = scratch[17:22]
    buffers = [
        scratch[22 + at * CHUNK_REFS : 22 + (at + 1) * CHUNK_REFS] for at in range(len(chunks))
    ]
    slots, local_cols, half_lat = held.shape
    fields, devices = plan.fields, plan.devices
    lat_count, lev_count = lax.axis_size("lat"), lax.axis_size("lev")
    lev_index, lat_index = lax.axis_index("lev"), lax.axis_index("lat")
    device = lev_index * lat_count + lat_index
    part_width = 4 * fields
    part_span = slots * part_width
    width = part_span * pack
    faces = width // BLK
    last = len(chunks) - 1
    direct = devices <= DIRECT
    greetings = hail(direct)
    inputs = [
        pltpu.make_async_copy(source, target, input_sems.at[at])
        for at, (source, target) in enumerate(
            ((deal_in, deal), (spec_in, spec_ref), (lengths_in, lengths), (mixing_in, mixing_ref))
        )
    ]
    for load in inputs:
        load.start()
    loads = []
    for at, (first, count) in enumerate(chunks):
        columns = pl.ds(first * devices, count * devices)
        load = pltpu.make_async_copy(
            legendre_ref.at[:, :, columns], held.at[:, :, columns], load_sems.at[at]
        )
        load.start()
        loads.append(load)
    inputs[0].wait()
    inputs[1].wait()
    odd, masks = column_masks(plan, deal, slots, local_cols)
    lefts = []
    for slot in range(slots):
        kept = jnp.concatenate([spec_ref[slot, 0], spec_ref[slot, 1]], axis=0).astype(jnp.float32)
        kept = kept * masks[slot]
        lefts.append(jnp.concatenate([kept, kept * odd], axis=0).astype(jnp.bfloat16))

    finished = []
    reduced, crossed, returned, shared = {}, {}, {}, {}

    def project(at):
        first, count = chunks[at]
        leaving, turned = buffers[at][0], buffers[at][7]
        each = count // pack
        loads[at].wait()
        sums = [
            jnp.dot(
                lefts[slot],
                held[slot, :, first * devices : (first + count) * devices],
                preferred_element_type=jnp.float32,
            )
            for slot in range(slots)
        ]
        for block in range(each * devices // BLK):
            piece = jnp.concatenate(
                [
                    value[:, part * each * devices + block * BLK : part * each * devices + (block + 1) * BLK]
                    for part in range(pack)
                    for value in sums
                ],
                axis=0,
            )
            for face in range(faces):
                turned[face, block * BLK : (block + 1) * BLK, :] = piece[face * BLK : (face + 1) * BLK].T
        for target in range(devices):
            for face in range(faces):
                leaving[target // lat_count, target % lat_count, :, face * BLK : (face + 1) * BLK] = (
                    turned[face, pl.ds(target, each, stride=devices), :].astype(jnp.bfloat16)
                )

    def start_reduce(at):
        leaving, arriving, lev_sems = (buffers[at][n] for n in (0, 1, 8))
        if at == 0 and direct:
            copies = send_all(
                lambda lev, lat: leaving.at[lev, lat], arriving.at[lev_index, lat_index], direct_sems.at[0]
            )
            arriving[lev_index, lat_index] = leaving[lev_index, lat_index]
        else:
            copies = send("lev", lambda peer: leaving.at[peer], arriving.at[lev_index], lev_sems.at[0])
        reduced[at] = copies
        finished.append(copies)

    def start_cross(at):
        count = chunks[at][1]
        arriving, summed, landed, turned, lat_sems = (buffers[at][n] for n in (1, 2, 3, 7, 9))
        each = count // pack
        total_of = jnp.stack(
            [
                jnp.concatenate(
                    [
                        turned[face, pl.ds(lev_index * lat_count + side, each, stride=devices), :]
                        for face in range(faces)
                    ],
                    axis=1,
                )
                for side in range(lat_count)
            ]
        )
        for peer in arrivals("lev", reduced[at]):
            total_of = total_of + arriving[peer].astype(jnp.float32)
        summed[...] = total_of.astype(jnp.bfloat16)
        crossed[at] = send("lat", lambda peer: summed.at[peer], landed.at[lat_index], lat_sems.at[0])
        landed[lat_index] = summed[lat_index]
        finished.append(crossed[at])

    def land(at):
        arriving, landed = buffers[at][1], buffers[at][3]
        if at == 0 and direct:
            for copy in reduced[at]:
                copy.wait_recv()
            blocks = []
            for side in range(lat_count):
                block = arriving[0, side].astype(jnp.float32)
                for lev in range(1, lev_count):
                    block = block + arriving[lev, side].astype(jnp.float32)
                blocks.append(block.astype(jnp.bfloat16).astype(jnp.float32))
            return blocks
        for _ in arrivals("lat", crossed[at]):
            pass
        return [landed[side].astype(jnp.float32) for side in range(lat_count)]

    def start_return(at):
        rows, back, gathered, lat_sems = (buffers[at][n] for n in (4, 5, 6, 9))
        if at == last and direct:
            shared[at] = send_all(
                lambda lev, lat: rows.at[lat], gathered.at[lev_index, lat_index], direct_sems.at[1]
            )
            gathered[lev_index, lat_index] = rows[lat_index]
            finished.append(shared[at])
        else:
            returned[at] = send("lat", lambda peer: rows.at[peer], back.at[lat_index], lat_sems.at[1])
            back[lat_index] = rows[lat_index]
            finished.append(returned[at])

    def pass_on(at):
        if at in shared:
            return
        back, gathered, lev_sems = (buffers[at][n] for n in (5, 6, 8))
        for _ in arrivals("lat", returned[at]):
            pass
        shared[at] = send("lev", lambda peer: back, gathered.at[lev_index], lev_sems.at[1])
        gathered[lev_index] = back[...]
        finished.append(shared[at])

    project(0)
    inputs[2].wait()
    inputs[3].wait()
    fill_constants(plan, deal, mixing_ref, keep, gather, placed_sign, mixer, sum_sign, spread, fold_keep)
    fill_tables(plan, device, lengths, deal, table, row_length)
    expect(greetings)
    start_reduce(0)
    if last > 0:
        project(1)
        start_reduce(1)
    for at in range(2, len(chunks)):
        project(at)
    if not direct:
        start_cross(0)
    if last > 0:
        start_cross(1)
    if last > 1:
        start_reduce(2)
    fill_products(plan, device, row_length, deal, products, weights)

    for at, (first, count) in enumerate(chunks):
        rows = buffers[at][4]
        each = count // pack
        blocks = land(at)
        values = jnp.concatenate(
            [
                jnp.concatenate(
                    [block[:, part * part_span : (part + 1) * part_span] for block in blocks], axis=1
                )
                for part in range(pack)
            ],
            axis=0,
        )
        values = values * weights[0, first : first + count]
        values_ref[first : first + count] = values
        place_coefficients(plan, first, values, keep, gather, placed_sign, mixer, left)
        groups = list(range(first // plan.share, (first + count) // plan.share))
        walk_circles(plan, groups, table, left, total)
        if 0 < at < last:
            pass_on(at - 1)
        size = 2 * plan.block
        result = fold_circles(
            plan,
            total[first // plan.share * size : (first + count) // plan.share * size, :],
            sum_sign,
            spread,
            fold_keep,
        )
        values = values_ref[first : first + count]
        for other in range(plan.waves):
            result = result + products[other, first : first + count] * rolled(plan, values, other)
        result = result * weights[1, first : first + count]
        for side in range(lat_count):
            rows[side] = jnp.concatenate(
                [
                    result[part * each : (part + 1) * each, side * part_span : (side + 1) * part_span]
                    for part in range(pack)
                ],
                axis=1,
            ).astype(jnp.bfloat16)
        start_return(at)
        if at + 2 <= last:
            start_cross(at + 2)
            if at + 3 <= last:
                start_reduce(at + 3)
    if last > 0:
        pass_on(last - 1)

    sums = [None] * slots
    for at, (first, count) in enumerate(chunks):
        gathered, turned = buffers[at][6], buffers[at][7]
        each = count // pack
        pass_on(at)
        for copy in shared[at]:
            copy.wait_recv()
        for source in range(devices):
            block = gathered[source // lat_count, source % lat_count].astype(jnp.float32)
            for face in range(faces):
                turned[face, pl.ds(source, each, stride=devices), :] = block[:, face * BLK : (face + 1) * BLK]
        sides = [turned[face].astype(jnp.bfloat16) for face in range(faces)]
        for slot in range(slots):
            for part in range(pack):
                lane = part * part_span + slot * part_width
                start = (first + part * each) * devices
                value = jnp.dot(
                    held[slot, :, start : start + each * devices],
                    sides[lane // BLK],
                    preferred_element_type=jnp.float32,
                )[:, lane % BLK : lane % BLK + part_width]
                sums[slot] = value if sums[slot] is None else sums[slot] + value
    odd, masks = column_masks(plan, deal, slots, local_cols)
    for slot in range(slots):
        flat = sums[slot].T
        out_ref[slot] = (flat[: 2 * fields] + odd * flat[2 * fields :]) * masks[slot]
    for copies in finished:
        for copy in copies:
            copy.wait_send()


def local(spec_in, legendre, pattern, deal_list, circle_lengths, mixing):
    lat_count, lev_count = lax.axis_size("lat"), lax.axis_size("lev")
    slots, local_cols, half_lat = legendre.shape
    fields, waves = spec_in.shape[2], deal_list.shape[0]
    plan = Plan(waves, fields, lat_count, lev_count, half_lat)
    span = 4 * slots * fields
    pack = max(1, BLK // span)
    chunks = plan.chunks(pack)
    vmem = pl.BlockSpec(memory_space=pltpu.VMEM)
    size, wide = 2 * plan.block, 4 * plan.images
    face = plan.face
    scratch = [
        pltpu.VMEM(legendre.shape, jnp.bfloat16),
        pltpu.SemaphoreType.DMA((len(chunks),)),
        pltpu.VMEM((plan.groups, wide, plan.depth), jnp.bfloat16),
        pltpu.VMEM((plan.groups, 5, plan.block, BLK), jnp.float32),
        pltpu.VMEM((plan.groups * size, face), jnp.float32),
        pltpu.VMEM((plan.rows, BLK), jnp.float32),
        pltpu.VMEM((waves, plan.rows, plan.lanes), jnp.float32),
        pltpu.VMEM((2, plan.rows, plan.lanes), jnp.float32),
        pltpu.VMEM((plan.rows, plan.lanes), jnp.float32),
        pltpu.VMEM((plan.hf, plan.lanes), jnp.float32),
        pltpu.VMEM((2 * plan.lanes, plan.depth), jnp.bfloat16),
        pltpu.VMEM((4, plan.images, plan.depth), jnp.float32),
        pltpu.VMEM((BLK, BLK), jnp.bfloat16),
        pltpu.VMEM((size, face), jnp.float32),
        pltpu.VMEM((2 * face, plan.lanes), jnp.bfloat16),
        pltpu.VMEM((size, plan.lanes), jnp.float32),
        pltpu.SemaphoreType.DMA((2, 2, min(plan.devices, DIRECT))),
        pltpu.SMEM(circle_lengths.shape, jnp.int32),
        pltpu.SMEM(deal_list.shape, jnp.int32),
        pltpu.VMEM(spec_in.shape, jnp.bfloat16),
        pltpu.VMEM(mixing.shape, jnp.bfloat16),
        pltpu.SemaphoreType.DMA((4,)),
    ]
    for _, count in chunks:
        scratch += chunk_scratch(count, pack, span * pack, lat_count, lev_count)
    product = pl.pallas_call(
        functools.partial(round_trip_kernel, plan, pack, chunks),
        out_shape=jax.ShapeDtypeStruct((slots, 2 * fields, local_cols), jnp.float32),
        in_specs=[pl.BlockSpec(memory_space=pltpu.HBM)] * 5,
        out_specs=vmem,
        scratch_shapes=scratch,
        compiler_params=pltpu.CompilerParams(
            collective_id=0, has_side_effects=True
        ),
    )(circle_lengths, deal_list, spec_in, legendre, mixing)
    return product.reshape(slots, 2, fields, local_cols)


def solution(mesh):
    return jax.shard_map(
        local,
        mesh=mesh,
        in_specs=(
            P("lat", None, None, "lev"),
            P("lat", "lev", None),
            P("lat", None, None),
            P(),
            P(),
            P(),
        ),
        out_specs=P("lat", None, None, "lev"),
        check_vma=False,
    )
```

```python
import functools
import math

import jax
import jax.numpy as jnp
from jax import lax
from jax.experimental import pallas as pl
from jax.experimental.pallas import tpu as pltpu
from jax.sharding import PartitionSpec as P

BLK = 128
SPAN = 2 * BLK
ACROSS = (((1,), (1,)), ((), ()))
STREAMS = 2
SPLIT = ((8, 10), (0, 4), (4, 8))
DIRECT = 64


def iota(shape, axis):
    return lax.broadcasted_iota(jnp.int32, shape, axis)


def unit(condition):
    return jnp.where(condition, 1.0, 0.0).astype(jnp.float32)


class Plan:
    def __init__(self, waves, fields, lat_count, lev_count, half_lat):
        self.waves, self.fields = waves, fields
        self.half_lat = half_lat
        self.devices = lat_count * lev_count
        self.rows = half_lat // self.devices
        self.hf = 2 * fields
        self.lanes = waves * 4 * fields
        self.share = max(
            n for n in range(1, self.rows + 1) if self.rows % n == 0 and (n == 1 or 4 * n * waves <= BLK)
        )
        self.groups = self.rows // self.share
        self.block = self.share * waves
        self.depth = 2 * self.block
        self.images = self.share * self.hf
        self.own = 4 * self.hf
        self.face = max(BLK, self.own)
        self.scale = (2.0 * waves) ** (-0.5)

    def tiles(self, group):
        needed = (group + 1) * self.share * self.devices + 5
        tiles = [(at, SPAN) for at in range(0, needed, SPAN)]
        if needed - tiles[-1][0] <= BLK:
            tiles[-1] = tiles[-1][0], BLK
        return tiles

    def inside(self, group, at, span):
        first = group * self.share * self.devices
        return at > 0 and at + span - 1 < 3 + first - first // 2

    def chunks(self, pack):
        least = pack
        while least * self.devices % (pack * BLK) or least % self.share:
            least += pack
        units = self.rows // least
        marks = [(units * start // 10 * least, units * stop // 10 * least) for start, stop in SPLIT]
        return [(start, stop - start) for start, stop in marks if stop > start]


def waves_at(deal, index, waves):
    out = jnp.zeros_like(index)
    for wave in range(waves):
        out = jnp.where(index == wave, deal[wave], out)
    return out


def circle_point(turns):
    quadrant = jnp.floor(4.0 * turns + 0.5)
    angle = (turns - 0.25 * quadrant) * (2.0 * math.pi)
    square = angle * angle
    sine = angle * (
        1.0 + square * (-1.0 / 6 + square * (1.0 / 120 + square * (-1.0 / 5040 + square * (1.0 / 362880))))
    )
    cosine = 1.0 + square * (
        -0.5 + square * (1.0 / 24 + square * (-1.0 / 720 + square * (1.0 / 40320 - square * (1.0 / 3628800))))
    )
    turned = (quadrant == 1.0) | (quadrant == 3.0)
    first, second = jnp.where(turned, sine, cosine), jnp.where(turned, cosine, sine)
    first = jnp.where((quadrant == 1.0) | (quadrant == 2.0), -first, first)
    second = jnp.where((quadrant == 2.0) | (quadrant == 3.0), -second, second)
    return first, second


def fill_tables(plan, device, lengths, deal, table, row_length):
    wave = waves_at(deal, iota((plan.block, BLK), 0) % plan.waves, plan.waves).astype(jnp.float32)
    product = wave * iota((plan.block, BLK), 1).astype(jnp.float32)
    member = iota((plan.block, BLK), 0) // plan.waves
    unroll = max(n for n in range(1, 6) if plan.groups % n == 0)

    def fill(step, carry):
        for near in range(unroll):
            group = step * unroll + near
            length = jnp.zeros((plan.block, BLK), jnp.float32)
            for each in range(plan.share):
                own = lengths[(group * plan.share + each) * plan.devices + device].astype(jnp.float32)
                length = jnp.where(member == each, own, length)
                row_length[pl.ds(group * plan.share + each, 1), :] = jnp.full((1, BLK), own, jnp.float32)
            inverse = 1.0 / length
            turned = product - jnp.floor(product * inverse) * length
            cosine, sine = circle_point(turned * inverse)
            last_cos, last_sin = cosine[:, BLK - 1 : BLK], sine[:, BLK - 1 : BLK]
            next_cos, next_sin = cosine[:, 1:2], sine[:, 1:2]
            table[group, 0] = cosine
            table[group, 1] = -sine
            table[group, 2] = jnp.broadcast_to(last_cos * next_cos - last_sin * next_sin, product.shape)
            table[group, 3] = jnp.broadcast_to(-last_sin * next_cos - last_cos * next_sin, product.shape)
            table[group, 4] = 0.25 * length + 0.5
        return carry

    lax.fori_loop(0, plan.groups // unroll, fill, 0)


def lane_waves(plan, deal):
    return waves_at(deal, iota((1, plan.lanes), 1) // (4 * plan.fields), plan.waves)


def live_rows(plan, device, deal):
    half_lat = plan.half_lat
    cut = lane_waves(plan, deal) * (half_lat // BLK) // (2 * half_lat)
    row = iota((plan.rows, 1), 0) * plan.devices + device
    return unit(row // BLK >= cut)


def image_sign(image, sine, odd):
    sign = jnp.ones(jnp.broadcast_shapes(sine.shape, odd.shape), jnp.float32)
    if image % 2:
        sign = sign * (1.0 - 2.0 * unit(sine))
    if image // 2:
        sign = sign * (1.0 - 2.0 * unit(odd))
    return sign


def fill_constants(plan, deal, mixing_ref, keep, gather, placed_sign, mixer, sum_sign, spread, fold_keep):
    waves, fields, hf, lanes = plan.waves, plan.fields, plan.hf, plan.lanes
    lane = iota((hf, lanes), 1)
    keep[...] = unit(lane // (2 * fields) % 2 * fields + lane % fields == iota((hf, lanes), 0))
    down, right = iota((lanes, plan.depth), 0), iota((lanes, plan.depth), 1)
    down_kind = down // fields % 2
    down_wave = down // (4 * fields)
    gather[...] = unit(
        (down_kind == right // plan.block) & (down_wave == right % waves)
    ).astype(jnp.bfloat16)
    right = iota((1, plan.depth), 1)
    mine = unit(iota((plan.images, 1), 0) // hf == right % plan.block // waves)
    odd = waves_at(deal, right % waves, waves) % 2 == 1
    sine = right // plan.block % 2 == 1
    for image in range(4):
        placed_sign[image] = mine * image_sign(image, sine, odd)
    pick = unit(iota((BLK, fields), 0) % fields == iota((BLK, fields), 1)).astype(jnp.bfloat16)
    half = lax.dot_general(
        pick, mixing_ref[...], ACROSS, preferred_element_type=jnp.float32
    ).astype(jnp.bfloat16)
    whole = lax.dot_general(half, pick, ACROSS, preferred_element_type=jnp.float32)
    same = iota((BLK, BLK), 0) // fields == iota((BLK, BLK), 1) // fields
    mixer[...] = jnp.where(same, whole, 0.0).astype(jnp.bfloat16)
    size, wide = sum_sign.shape
    down, right = iota((size, wide), 0), iota((size, wide), 1)
    each = down // (2 * waves)
    lane = each * plan.own // plan.face * plan.face + right
    odd = waves_at(deal, down % waves, waves) % 2 == 1
    sine = down // waves % 2 == 1
    sign = jnp.zeros((size, wide), jnp.float32)
    for image in range(4):
        sign = jnp.where(lane % plan.own // hf == image, image_sign(image, sine, odd), sign)
    sum_sign[...] = sign * unit(each == lane // plan.own)
    down, right = iota((2 * wide, lanes), 0), iota((2 * wide, lanes), 1)
    spread[...] = unit(
        down % hf == right // (2 * fields) % 2 * fields + right % fields
    ).astype(jnp.bfloat16)
    down, right = iota((size, lanes), 0), iota((size, lanes), 1)
    fold_keep[...] = unit(
        (down // waves % 2 == right // fields % 2) & (down % waves == right // (4 * fields))
    )


def fill_products(plan, device, row_length, deal, products, weights):
    length = jnp.concatenate([row_length[...]] * (plan.lanes // BLK), axis=1)
    wave = lane_waves(plan, deal).astype(jnp.float32)
    part = 1.0 - 2.0 * unit(iota((1, plan.lanes), 1) // plan.fields % 2 == 1)
    inverse, half = 1.0 / length, (0.5 * plan.scale) * length

    def whole(turns):
        return unit(turns == length * jnp.floor(turns * inverse + 0.5))

    for other in range(plan.waves):
        partner = rolled(plan, wave, other)
        products[other] = half * (whole(wave - partner) + part * whole(wave + partner))
    row = (iota((plan.rows, 1), 0) * plan.devices + device).astype(jnp.float32)
    weight = jnp.sin(math.pi * (row + 0.5) / (2 * plan.half_lat)) / jnp.sqrt(row_length[...])
    weights[0] = live_rows(plan, device, deal)
    weights[1] = weights[0] * jnp.concatenate([weight] * (plan.lanes // BLK), axis=1)


def rolled(plan, source, other):
    at = other * 4 * plan.fields
    return jnp.concatenate([source[:, at:], source[:, :at]], axis=1) if at else source


def place_coefficients(plan, first, values, keep, gather, placed_sign, mixer, left):
    rows = values.shape[0]
    narrow = values.astype(jnp.bfloat16)
    mixed = plan.scale * jnp.concatenate(
        [
            jnp.dot(narrow[:, at : at + BLK], mixer[...], preferred_element_type=jnp.float32)
            for at in range(0, plan.lanes, BLK)
        ],
        axis=1,
    )
    spread = (mixed[:, None, :] * keep[...][None]).reshape(rows * plan.hf, plan.lanes).astype(jnp.bfloat16)
    placed = jnp.dot(spread, gather[...], preferred_element_type=jnp.float32)
    for group in range(rows // plan.share):
        for each in range(plan.share):
            at = (group * plan.share + each) * plan.hf
            for image in range(4):
                to = each * plan.own + image * plan.hf
                left[first // plan.share + group, to : to + plan.hf, :] = (
                    placed[at : at + plan.hf] * placed_sign[image, each * plan.hf : (each + 1) * plan.hf, :]
                ).astype(jnp.bfloat16)


def walk_circles(plan, groups, table, left, total):
    position = iota((1, SPAN), 1).astype(jnp.float32)

    def phases(group, at, span, cos_now, sin_now):
        step_cos, step_sin = table[group, 2], table[group, 3]
        cosines, sines = [], []
        for _ in range(span // BLK):
            cosines.append(cos_now)
            sines.append(sin_now)
            cos_now, sin_now = (
                cos_now * step_cos - sin_now * step_sin,
                sin_now * step_cos + cos_now * step_sin,
            )
        cosine, sine = jnp.concatenate(cosines, axis=1), jnp.concatenate(sines, axis=1)
        near, far = cosine.astype(jnp.bfloat16), sine.astype(jnp.bfloat16)
        weights = jnp.concatenate([near, far], axis=0)
        if plan.inside(group, at, span):
            return cos_now, sin_now, weights, weights[: 2 * plan.block]
        limit = jnp.concatenate([table[group, 4]] * (span // BLK), axis=1)
        share = jnp.clip(limit - (position[:, :span] + float(at)), 0.0, 1.0)
        if at == 0:
            share = share * jnp.where(position[:, :span] == 0.0, 0.5, 1.0)
        shared = jnp.concatenate([cosine * share, sine * share], axis=0).astype(jnp.bfloat16)
        return cos_now, sin_now, weights, shared

    streams = [[] for _ in range(STREAMS)]
    for group in sorted(groups, key=lambda group: -len(plan.tiles(group))):
        min(streams, key=len).extend((group, at, span) for at, span in plan.tiles(group))
    state, sums, waiting = {}, {}, []

    def finish():
        for group, shared, grid in waiting:
            extra = lax.dot_general(
                shared,
                jnp.tanh(grid).astype(jnp.bfloat16),
                ACROSS,
                preferred_element_type=jnp.float32,
            )
            parts = []
            for each in range(plan.share):
                side = each * plan.own // plan.face * plan.face
                for row in (each * plan.waves, plan.block + each * plan.waves):
                    parts.append(extra[row : row + plan.waves, side : side + plan.face])
            if group in sums:
                parts = [old + new for old, new in zip(sums[group], parts)]
            sums[group] = parts
        waiting.clear()

    for step in range(max(len(stream) for stream in streams)):
        started = []
        for stream in streams:
            if step < len(stream):
                group, at, span = stream[step]
                if group not in state:
                    state[group] = table[group, 0], table[group, 1]
                cos_now, sin_now, weights, shared = phases(group, at, span, *state[group])
                state[group] = cos_now, sin_now
                grid = jnp.dot(left[group], weights, preferred_element_type=jnp.float32)
                started.append((group, shared, grid))
        finish()
        waiting.extend(started)
    finish()
    size = 2 * plan.block
    for group in groups:
        for at, part in enumerate(sums[group]):
            total[group * size + at * plan.waves : group * size + (at + 1) * plan.waves, :] = part


def fold_circles(plan, sums, sum_sign, spread, fold_keep):
    size, wide = sum_sign.shape
    count = sums.shape[0] // size
    signed = (sums.reshape(count, size, wide) * sum_sign[...][None]).reshape(count * size, wide)
    high = signed.astype(jnp.bfloat16)
    low = (signed - high.astype(jnp.float32)).astype(jnp.bfloat16)
    folded = jnp.dot(
        jnp.concatenate([high, low], axis=1), spread[...], preferred_element_type=jnp.float32
    )
    kept = (folded.reshape(count, size, plan.lanes) * fold_keep[...][None]).reshape(
        count * plan.share, 2, plan.waves, plan.lanes
    )
    return jnp.sum(jnp.sum(kept, axis=1), axis=1)


def column_masks(plan, deal, slots, local_cols):
    column = iota((1, local_cols), 1) + lax.axis_index("lev") * local_cols
    odd = (1 - 2 * (column % 2)).astype(jnp.float32)
    masks = []
    for slot in range(slots):
        wave = deal[lax.axis_index("lat") * slots + slot]
        masks.append(unit(column // BLK * BLK <= plan.half_lat - 1 - wave))
    return odd, masks


def peers_of(axis):
    count = lax.axis_size(axis)
    return [lax.rem(lax.axis_index(axis) + off, count) for off in range(1, count)]


def expect(total):
    pl.semaphore_wait(pltpu.get_barrier_semaphore(), total)


def others(count):
    lat_count = lax.axis_size("lat")
    me = lax.axis_index("lev") * lat_count + lax.axis_index("lat")
    for off in range(1, count):
        peer = lax.rem(me + off, count)
        yield {"lat": lax.rem(peer, lat_count), "lev": lax.div(peer, lat_count)}


def hail(direct):
    barrier = pltpu.get_barrier_semaphore()
    if direct:
        peers = list(others(lax.axis_size("lat") * lax.axis_size("lev")))
    else:
        peers = [{axis: peer} for axis in ("lat", "lev") for peer in peers_of(axis)]
    for peer in peers:
        pl.semaphore_signal(barrier, inc=1, device_id=peer, device_id_type=pl.DeviceIdType.MESH)
    return len(peers)


def send_all(sources, target, sems):
    copies = []
    for step, peer in enumerate(others(lax.axis_size("lat") * lax.axis_size("lev"))):
        copy = pltpu.make_async_remote_copy(
            src_ref=sources(peer["lev"], peer["lat"]),
            dst_ref=target,
            send_sem=sems.at[0, step],
            recv_sem=sems.at[1, step],
            device_id=peer,
            device_id_type=pl.DeviceIdType.MESH,
        )
        copy.start()
        copies.append(copy)
    return copies


def send(axis, sources, target, sems):
    copies = []
    for step, peer in enumerate(peers_of(axis)):
        copy = pltpu.make_async_remote_copy(
            src_ref=sources(peer),
            dst_ref=target,
            send_sem=sems.at[0, step],
            recv_sem=sems.at[1, step],
            device_id={axis: peer},
            device_id_type=pl.DeviceIdType.MESH,
        )
        copy.start()
        copies.append(copy)
    return copies


def arrivals(axis, copies):
    count, index = lax.axis_size(axis), lax.axis_index(axis)
    for off, copy in enumerate(copies, 1):
        copy.wait_recv()
        yield lax.rem(index + count - off, count)


def chunk_scratch(count, pack, width, lat_count, lev_count):
    block = (lat_count, count // pack, width)
    devices = lat_count * lev_count
    return [
        pltpu.VMEM((lev_count,) + block, jnp.bfloat16),
        pltpu.VMEM((lev_count,) + block, jnp.bfloat16),
        pltpu.VMEM(block, jnp.bfloat16),
        pltpu.VMEM(block, jnp.bfloat16),
        pltpu.VMEM(block, jnp.bfloat16),
        pltpu.VMEM(block, jnp.bfloat16),
        pltpu.VMEM((lev_count,) + block, jnp.bfloat16),
        pltpu.VMEM((width // BLK, count // pack * devices, BLK), jnp.float32),
        pltpu.SemaphoreType.DMA((2, 2, lev_count)),
        pltpu.SemaphoreType.DMA((2, 2, lat_count)),
    ]


CHUNK_REFS = 10


def round_trip_kernel(
    plan, pack, chunks, lengths_in, deal_in, spec_in, legendre_ref, mixing_in, out_ref, *scratch
):
    held, load_sems, left, table, total, row_length, products, weights, values_ref = scratch[:9]
    keep, gather, placed_sign, mixer, sum_sign, spread, fold_keep, direct_sems = scratch[9:17]
    lengths, deal, spec_ref, mixing_ref, input_sems = scratch[17:22]
    buffers = [
        scratch[22 + at * CHUNK_REFS : 22 + (at + 1) * CHUNK_REFS] for at in range(len(chunks))
    ]
    slots, local_cols, half_lat = held.shape
    fields, devices = plan.fields, plan.devices
    lat_count, lev_count = lax.axis_size("lat"), lax.axis_size("lev")
    lev_index, lat_index = lax.axis_index("lev"), lax.axis_index("lat")
    device = lev_index * lat_count + lat_index
    part_width = 4 * fields
    part_span = slots * part_width
    width = part_span * pack
    faces = width // BLK
    last = len(chunks) - 1
    direct = devices <= DIRECT
    greetings = hail(direct)
    inputs = [
        pltpu.make_async_copy(source, target, input_sems.at[at])
        for at, (source, target) in enumerate(
            ((deal_in, deal), (spec_in, spec_ref), (lengths_in, lengths), (mixing_in, mixing_ref))
        )
    ]
    for load in inputs:
        load.start()
    loads = []
    for at, (first, count) in enumerate(chunks):
        columns = pl.ds(first * devices, count * devices)
        load = pltpu.make_async_copy(
            legendre_ref.at[:, :, columns], held.at[:, :, columns], load_sems.at[at]
        )
        load.start()
        loads.append(load)
    inputs[0].wait()
    inputs[1].wait()
    odd, masks = column_masks(plan, deal, slots, local_cols)
    lefts = []
    for slot in range(slots):
        kept = jnp.concatenate([spec_ref[slot, 0], spec_ref[slot, 1]], axis=0).astype(jnp.float32)
        kept = kept * masks[slot]
        lefts.append(jnp.concatenate([kept, kept * odd], axis=0).astype(jnp.bfloat16))

    finished = []
    reduced, crossed, returned, shared = {}, {}, {}, {}

    def project(at):
        first, count = chunks[at]
        leaving, turned = buffers[at][0], buffers[at][7]
        each = count // pack
        loads[at].wait()
        sums = [
            jnp.dot(
                lefts[slot],
                held[slot, :, first * devices : (first + count) * devices],
                preferred_element_type=jnp.float32,
            )
            for slot in range(slots)
        ]
        for block in range(each * devices // BLK):
            piece = jnp.concatenate(
                [
                    value[:, part * each * devices + block * BLK : part * each * devices + (block + 1) * BLK]
                    for part in range(pack)
                    for value in sums
                ],
                axis=0,
            )
            for face in range(faces):
                turned[face, block * BLK : (block + 1) * BLK, :] = piece[face * BLK : (face + 1) * BLK].T
        for target in range(devices):
            for face in range(faces):
                leaving[target // lat_count, target % lat_count, :, face * BLK : (face + 1) * BLK] = (
                    turned[face, pl.ds(target, each, stride=devices), :].astype(jnp.bfloat16)
                )

    def start_reduce(at):
        leaving, arriving, lev_sems = (buffers[at][n] for n in (0, 1, 8))
        if at == 0 and direct:
            copies = send_all(
                lambda lev, lat: leaving.at[lev, lat], arriving.at[lev_index, lat_index], direct_sems.at[0]
            )
            arriving[lev_index, lat_index] = leaving[lev_index, lat_index]
        else:
            copies = send("lev", lambda peer: leaving.at[peer], arriving.at[lev_index], lev_sems.at[0])
        reduced[at] = copies
        finished.append(copies)

    def start_cross(at):
        count = chunks[at][1]
        arriving, summed, landed, turned, lat_sems = (buffers[at][n] for n in (1, 2, 3, 7, 9))
        each = count // pack
        total_of = jnp.stack(
            [
                jnp.concatenate(
                    [
                        turned[face, pl.ds(lev_index * lat_count + side, each, stride=devices), :]
                        for face in range(faces)
                    ],
                    axis=1,
                )
                for side in range(lat_count)
            ]
        )
        for peer in arrivals("lev", reduced[at]):
            total_of = total_of + arriving[peer].astype(jnp.float32)
        summed[...] = total_of.astype(jnp.bfloat16)
        crossed[at] = send("lat", lambda peer: summed.at[peer], landed.at[lat_index], lat_sems.at[0])
        landed[lat_index] = summed[lat_index]
        finished.append(crossed[at])

    def land(at):
        arriving, landed = buffers[at][1], buffers[at][3]
        if at == 0 and direct:
            for copy in reduced[at]:
                copy.wait_recv()
            blocks = []
            for side in range(lat_count):
                block = arriving[0, side].astype(jnp.float32)
                for lev in range(1, lev_count):
                    block = block + arriving[lev, side].astype(jnp.float32)
                blocks.append(block.astype(jnp.bfloat16).astype(jnp.float32))
            return blocks
        for _ in arrivals("lat", crossed[at]):
            pass
        return [landed[side].astype(jnp.float32) for side in range(lat_count)]

    def start_return(at):
        rows, back, gathered, lat_sems = (buffers[at][n] for n in (4, 5, 6, 9))
        if at == last and direct:
            shared[at] = send_all(
                lambda lev, lat: rows.at[lat], gathered.at[lev_index, lat_index], direct_sems.at[1]
            )
            gathered[lev_index, lat_index] = rows[lat_index]
            finished.append(shared[at])
        else:
            returned[at] = send("lat", lambda peer: rows.at[peer], back.at[lat_index], lat_sems.at[1])
            back[lat_index] = rows[lat_index]
            finished.append(returned[at])

    def pass_on(at):
        if at in shared:
            return
        back, gathered, lev_sems = (buffers[at][n] for n in (5, 6, 8))
        for _ in arrivals("lat", returned[at]):
            pass
        shared[at] = send("lev", lambda peer: back, gathered.at[lev_index], lev_sems.at[1])
        gathered[lev_index] = back[...]
        finished.append(shared[at])

    project(0)
    inputs[2].wait()
    inputs[3].wait()
    fill_constants(plan, deal, mixing_ref, keep, gather, placed_sign, mixer, sum_sign, spread, fold_keep)
    fill_tables(plan, device, lengths, deal, table, row_length)
    expect(greetings)
    start_reduce(0)
    if last > 0:
        project(1)
        start_reduce(1)
    for at in range(2, len(chunks)):
        project(at)
    if not direct:
        start_cross(0)
    if last > 0:
        start_cross(1)
    if last > 1:
        start_reduce(2)
    fill_products(plan, device, row_length, deal, products, weights)

    for at, (first, count) in enumerate(chunks):
        rows = buffers[at][4]
        each = count // pack
        blocks = land(at)
        values = jnp.concatenate(
            [
                jnp.concatenate(
                    [block[:, part * part_span : (part + 1) * part_span] for block in blocks], axis=1
                )
                for part in range(pack)
            ],
            axis=0,
        )
        values = values * weights[0, first : first + count]
        values_ref[first : first + count] = values
        place_coefficients(plan, first, values, keep, gather, placed_sign, mixer, left)
        groups = list(range(first // plan.share, (first + count) // plan.share))
        walk_circles(plan, groups, table, left, total)
        if 0 < at < last:
            pass_on(at - 1)
        size = 2 * plan.block
        result = fold_circles(
            plan,
            total[first // plan.share * size : (first + count) // plan.share * size, :],
            sum_sign,
            spread,
            fold_keep,
        )
        values = values_ref[first : first + count]
        for other in range(plan.waves):
            result = result + products[other, first : first + count] * rolled(plan, values, other)
        result = result * weights[1, first : first + count]
        for side in range(lat_count):
            rows[side] = jnp.concatenate(
                [
                    result[part * each : (part + 1) * each, side * part_span : (side + 1) * part_span]
                    for part in range(pack)
                ],
                axis=1,
            ).astype(jnp.bfloat16)
        start_return(at)
        if at + 2 <= last:
            start_cross(at + 2)
            if at + 3 <= last:
                start_reduce(at + 3)
    if last > 0:
        pass_on(last - 1)

    sums = [None] * slots
    for at, (first, count) in enumerate(chunks):
        gathered, turned = buffers[at][6], buffers[at][7]
        each = count // pack
        pass_on(at)
        for copy in shared[at]:
            copy.wait_recv()
        for source in range(devices):
            block = gathered[source // lat_count, source % lat_count].astype(jnp.float32)
            for face in range(faces):
                turned[face, pl.ds(source, each, stride=devices), :] = block[:, face * BLK : (face + 1) * BLK]
        sides = [turned[face].astype(jnp.bfloat16) for face in range(faces)]
        for slot in range(slots):
            for part in range(pack):
                lane = part * part_span + slot * part_width
                start = (first + part * each) * devices
                value = jnp.dot(
                    held[slot, :, start : start + each * devices],
                    sides[lane // BLK],
                    preferred_element_type=jnp.float32,
                )[:, lane % BLK : lane % BLK + part_width]
                sums[slot] = value if sums[slot] is None else sums[slot] + value
    odd, masks = column_masks(plan, deal, slots, local_cols)
    for slot in range(slots):
        flat = sums[slot].T
        out_ref[slot] = (flat[: 2 * fields] + odd * flat[2 * fields :]) * masks[slot]
    for copies in finished:
        for copy in copies:
            copy.wait_send()


def local(spec_in, legendre, pattern, deal_list, circle_lengths, mixing):
    lat_count, lev_count = lax.axis_size("lat"), lax.axis_size("lev")
    slots, local_cols, half_lat = legendre.shape
    fields, waves = spec_in.shape[2], deal_list.shape[0]
    plan = Plan(waves, fields, lat_count, lev_count, half_lat)
    span = 4 * slots * fields
    pack = max(1, BLK // span)
    chunks = plan.chunks(pack)
    vmem = pl.BlockSpec(memory_space=pltpu.VMEM)
    size, wide = 2 * plan.block, 4 * plan.images
    face = plan.face
    scratch = [
        pltpu.VMEM(legendre.shape, jnp.bfloat16),
        pltpu.SemaphoreType.DMA((len(chunks),)),
        pltpu.VMEM((plan.groups, wide, plan.depth), jnp.bfloat16),
        pltpu.VMEM((plan.groups, 5, plan.block, BLK), jnp.float32),
        pltpu.VMEM((plan.groups * size, face), jnp.float32),
        pltpu.VMEM((plan.rows, BLK), jnp.float32),
        pltpu.VMEM((waves, plan.rows, plan.lanes), jnp.float32),
        pltpu.VMEM((2, plan.rows, plan.lanes), jnp.float32),
        pltpu.VMEM((plan.rows, plan.lanes), jnp.float32),
        pltpu.VMEM((plan.hf, plan.lanes), jnp.float32),
        pltpu.VMEM((plan.lanes, plan.depth), jnp.bfloat16),
        pltpu.VMEM((4, plan.images, plan.depth), jnp.float32),
        pltpu.VMEM((BLK, BLK), jnp.bfloat16),
        pltpu.VMEM((size, face), jnp.float32),
        pltpu.VMEM((2 * face, plan.lanes), jnp.bfloat16),
        pltpu.VMEM((size, plan.lanes), jnp.float32),
        pltpu.SemaphoreType.DMA((2, 2, min(plan.devices, DIRECT))),
        pltpu.SMEM(circle_lengths.shape, jnp.int32),
        pltpu.SMEM(deal_list.shape, jnp.int32),
        pltpu.VMEM(spec_in.shape, jnp.bfloat16),
        pltpu.VMEM(mixing.shape, jnp.bfloat16),
        pltpu.SemaphoreType.DMA((4,)),
    ]
    for _, count in chunks:
        scratch += chunk_scratch(count, pack, span * pack, lat_count, lev_count)
    product = pl.pallas_call(
        functools.partial(round_trip_kernel, plan, pack, chunks),
        out_shape=jax.ShapeDtypeStruct((slots, 2 * fields, local_cols), jnp.float32),
        in_specs=[pl.BlockSpec(memory_space=pltpu.HBM)] * 5,
        out_specs=vmem,
        scratch_shapes=scratch,
        compiler_params=pltpu.CompilerParams(
            collective_id=0, has_side_effects=True
        ),
    )(circle_lengths, deal_list, spec_in, legendre, mixing)
    return product.reshape(slots, 2, fields, local_cols)


def solution(mesh):
    return jax.shard_map(
        local,
        mesh=mesh,
        in_specs=(
            P("lat", None, None, "lev"),
            P("lat", "lev", None),
            P("lat", None, None),
            P(),
            P(),
            P(),
        ),
        out_specs=P("lat", None, None, "lev"),
        check_vma=False,
    )
```
